256 devices in a mesh: ctx: 16 (over z_hi, y), head: 16 (over x, z_lo, core).
Axes of the slice: x: 4, y: 4, z: 8 (z_hi: 4, z_lo: 2; z = z_hi * 2 + z_lo), core: 2. Of those that a mesh axis runs over, the one named last changes fastest.
Arguments:
- queries: bfloat16 [4096, 16384], P('ctx', 'head'), may hold values from -10 to 10
- key_states: bfloat16 [4096, 1024], P('ctx'), may hold values from -10 to 10
- value_states: bfloat16 [4096, 1024], P('ctx'), may hold values from -6 to 6
- vertical_blocks: int32 [128, 4], P('head'), may hold values from 0 to 31, as said below
- slash_offsets: int32 [128, 4], P('head'), may hold values from 0 to 31, as said below
- positions: int32 [4096], P('ctx'), may hold values from 0 to 32767, as said below
- out_weight: bfloat16 [16384, 16384], P('head', 'ctx'), may hold values from -0.25 to 0.25
Outputs:
- projected: bfloat16 [4096, 16384], P('head', 'ctx')
The draws below stay inside these ranges and needn't reach their ends.
Inputs may be any that keep to these rules, and one draw needn't show every extreme that they name: `vertical_blocks`: each head's 4 vertical blocks are distinct. `slash_offsets`: each head's 4 offsets are distinct and the first of them is 0. `positions`: positions rise by one inside each block of 128 tokens; block b starts at a multiple of 128 at or after b * 1024 and before (b + 1) * 1024.
All inputs are finite; a program needn't handle non-finite values.
Results may differ from the reference program's by a relative error of at most 0.025.
Values may be sent and summed in bfloat16 or wider, within the bound.
A program may use at most 64 MiB of HBM per device.

```python
import math
import jax
import jax.numpy as jnp
from jax import lax

D = 16384
HD = 128
GROUP = 16
BLK = 128
NV = 4
NS = 4
PROMPT = 32768
HEADS = 128
KV_HEADS = 8
TOKENS = 4096
NB = 32
N_HEAD = 16


def draw_queries(key, part):
    noise_key = jax.random.fold_in(key, 1)
    base = jnp.clip(2.0 * jax.random.normal(noise_key, (TOKENS, HEADS, HD), jnp.float32), -10.0, 10.0)
    return base.reshape(TOKENS, HEADS * HD).astype(jnp.bfloat16)


def draw_key_states(key, part):
    noise_key = jax.random.fold_in(key, 2)
    base = jnp.clip(jax.random.normal(noise_key, (TOKENS, KV_HEADS, HD), jnp.float32), -6.0, 6.0)
    return base.reshape(TOKENS, KV_HEADS * HD).astype(jnp.bfloat16)


def block_order(one_key):
    return jax.random.permutation(one_key, NB)


def offset_order(one_key):
    return jax.random.permutation(one_key, NB - 1)


def draw_vertical_blocks(key, part):
    head_keys = jax.random.split(jax.random.fold_in(key, 3), HEADS)
    orders = jax.vmap(block_order)(head_keys)
    return orders[:, :NV].astype(jnp.int32)


def draw_slash_offsets(key, part):
    head_keys = jax.random.split(jax.random.fold_in(key, 4), HEADS)
    orders = jax.vmap(offset_order)(head_keys)[:, :NS - 1] + 1
    leading = jnp.zeros((HEADS, 1), jnp.int32)
    return jnp.concatenate([leading, orders.astype(jnp.int32)], axis=1)


def draw_positions(key, part):
    stride = PROMPT // NB
    offsets = jax.random.randint(jax.random.fold_in(key, 5), (NB,), 0, stride // BLK) * BLK
    starts = jnp.arange(NB, dtype=jnp.int32) * stride + offsets
    return (jnp.repeat(starts, BLK) + jnp.tile(jnp.arange(BLK, dtype=jnp.int32), NB)).astype(jnp.int32)


def steps_of(stream_key, extent, cuts, low, high):
    loudness, own = 1.0, jax.random.fold_in(stream_key, 6)
    for position, shards_of in cuts:
        heights = jnp.exp(jax.random.uniform(jax.random.fold_in(own, position), (shards_of,), jnp.float32, low / len(cuts), high / len(cuts)))
        loudness = loudness * jnp.repeat(heights, extent[position] // shards_of).reshape([-1 if axis == position else 1 for axis in range(len(extent))])
    return loudness


def scatter_about(key, shape, scale, reach, shards=(), kind=jnp.bfloat16):
    drawn = jax.random.normal(key, shape, jnp.float32) * scale
    if len(shards) > 0:
        drawn = steps_of(key, shape, shards, -0.22, 0.18) * drawn
    return jnp.clip(drawn, min=-reach, max=reach).astype(kind)


def setup_inputs(seed: int = 0) -> dict:
    arg_keys = jax.random.split(jax.random.key(seed), 8)
    return {
        "queries": draw_queries(jax.random.fold_in(arg_keys[7], 71), 0),
        "key_states": draw_key_states(jax.random.fold_in(arg_keys[7], 71), 0),
        "value_states": scatter_about(arg_keys[2], (TOKENS, KV_HEADS * HD), 1.0, 6.0, ((0, 16),)),
        "vertical_blocks": draw_vertical_blocks(jax.random.fold_in(arg_keys[7], 71), 0),
        "slash_offsets": draw_slash_offsets(jax.random.fold_in(arg_keys[7], 71), 0),
        "positions": draw_positions(jax.random.fold_in(arg_keys[7], 71), 0),
        "out_weight": scatter_about(arg_keys[6], (HEADS * HD, D), (HEADS * HD // 32) ** -0.5, 0.25, ((0, 16), (1, 16))),
    }


def rotate_heads(states, positions):
    half_width = states.shape[-1] // 2
    exponents = jnp.arange(half_width, dtype=jnp.float32) * (2.0 / states.shape[-1])
    inverse_freq = 500000.0 ** (-exponents)
    angles = positions.astype(jnp.float32)[:, None] * inverse_freq[None, :]
    cosine = jnp.cos(angles)[:, None, :]
    sine_part = jnp.sin(angles)[:, None, :]
    front_half = states[..., :half_width]
    back_half = states[..., half_width:]
    return jnp.concatenate([front_half * cosine - back_half * sine_part, back_half * cosine + front_half * sine_part], axis=-1)

def reference(queries, key_states, value_states, vertical_blocks, slash_offsets, positions, out_weight):
    query_rot = rotate_heads(queries.astype(jnp.float32).reshape(TOKENS, HEADS, HD), positions).astype(jnp.bfloat16)
    key_rot = rotate_heads(key_states.astype(jnp.float32).reshape(TOKENS, KV_HEADS, HD), positions).astype(jnp.bfloat16)
    value_heads = value_states.reshape(TOKENS, KV_HEADS, HD)
    block_index = jnp.arange(NB, dtype=jnp.int32)
    token_block = jnp.arange(TOKENS, dtype=jnp.int32) // BLK
    causal_pairs = jnp.arange(TOKENS)[None, :] <= jnp.arange(TOKENS)[:, None]

    def one_head(head):
        group_id = head // GROUP
        vertical_row = lax.dynamic_index_in_dim(vertical_blocks, head, 0, keepdims=False)
        slash_row = lax.dynamic_index_in_dim(slash_offsets, head, 0, keepdims=False)
        later = block_index[:, None]
        earlier = block_index[None, :]
        in_vertical = jnp.any(earlier[..., None] == vertical_row[None, None, :], axis=-1)
        in_slash = jnp.any((later - earlier)[..., None] == slash_row[None, None, :], axis=-1)
        block_mask = (earlier <= later) & (in_vertical | in_slash)
        token_mask = block_mask[token_block][:, token_block] & causal_pairs
        query_head = lax.dynamic_index_in_dim(query_rot, head, 1, keepdims=False)
        key_head = lax.dynamic_index_in_dim(key_rot, group_id, 1, keepdims=False)
        value_head = lax.dynamic_index_in_dim(value_heads, group_id, 1, keepdims=False)
        scores = jnp.dot(query_head, key_head.T, preferred_element_type=jnp.float32) / math.sqrt(HD)
        masked = jnp.where(token_mask, scores, -1e+30)
        row_max = lax.optimization_barrier(jnp.max(masked, axis=1, keepdims=True))
        exponentials = jnp.exp(masked - row_max)
        weights = (exponentials / lax.optimization_barrier(jnp.sum(exponentials, axis=1, keepdims=True))).astype(jnp.bfloat16)
        return jnp.dot(weights, value_head, preferred_element_type=jnp.float32).astype(jnp.bfloat16)
    per_head = lax.map(one_head, jnp.arange(HEADS, dtype=jnp.int32))
    head_out = jnp.transpose(per_head, (1, 0, 2)).reshape(TOKENS, HEADS * HD)
    group_rows = HEADS * HD // N_HEAD
    accumulated = jnp.zeros((TOKENS, D), jnp.float32)
    for group_id in range(N_HEAD):
        partial_value = jnp.dot(head_out[:, group_id * group_rows:(group_id + 1) * group_rows], out_weight[group_id * group_rows:(group_id + 1) * group_rows], preferred_element_type=jnp.float32).astype(jnp.bfloat16)
        partial_value = lax.optimization_barrier(partial_value)
        accumulated = accumulated + partial_value.astype(jnp.float32)
    return accumulated.astype(jnp.bfloat16)
```

```python
import math

import jax
import jax.numpy as jnp
from jax import lax
from jax.experimental import pallas as pl
from jax.experimental.pallas import tpu as pltpu
from jax.sharding import PartitionSpec as P

HD = 128
GROUP = 16
BLK = 128
MESH = pl.DeviceIdType.MESH


def place():
    ctx = lax.axis_index("ctx")
    head = lax.axis_index("head")
    return ctx // 4, ctx % 4, head // 4, (head // 2) % 2, head % 2


def device(zh, y, x, zl, core):
    return {"ctx": zh * 4 + y, "head": x * 4 + zl * 2 + core}


def remote(src, dst, send, recv, where):
    return pltpu.make_async_remote_copy(
        src_ref=src, dst_ref=dst, send_sem=send, recv_sem=recv, device_id=where, device_id_type=MESH
    )


def project_kernel(
    own_ref, w_ref, out_ref, acts, weights, sib_out, sib_in, held, tree_out, leaf_in, root_in,
    last_out, last_in, w_sem, w_send, w_recv, act_recv, z_send, y_send, sib_send, sib_recv,
    leaf_send, leaf_recv, root_send, root_recv, last_send, last_recv,
):
    zh, y, x, zl, core = place()
    mate = 3 - y
    pair = y + 1 - 2 * (y % 2)
    z_up = device((zh + 1) % 4, y, x, zl, core)
    z_down = device((zh + 3) % 4, y, x, zl, core)
    y_mate = device(zh, mate, x, zl, core)
    y_pair = device(zh, pair, x, zl, core)
    x_up = device(zh, y, (x + 1) % 4, zl, core)
    x_down = device(zh, y, (x + 3) % 4, zl, core)
    sibling = device(zh, y, x, zl, 1 - core)
    half = sib_out.shape[2]
    rows = acts.shape[1] // 2
    tiles = half // 256

    token_row = zl * 2 + core
    near = jnp.where((token_row == y) | (token_row == 3 - y), 1, 0)
    source_row = jnp.where(near == 1, y, pair)

    barrier = pltpu.get_barrier_semaphore()

    def greet(where):
        pl.semaphore_signal(barrier, inc=1, device_id=where, device_id_type=MESH)

    for where in (z_up, z_down, y_mate, y_pair, x_up, x_down, sibling):
        greet(where)
    for zs in range(2):
        for cs in range(2):
            @pl.when((near == 0) | (zs != zl) | (cs != core))
            def _():
                greet(device(zh, source_row, x, zs, cs))
    pl.semaphore_wait(barrier, 11 - near)

    def act_copy(src_slot, dst_slot, part, send, where):
        return remote(
            acts.at[src_slot, pl.ds(part * rows, rows)], acts.at[dst_slot, pl.ds(part * rows, rows)],
            send, act_recv.at[dst_slot, part], where,
        )

    def act_wait(slot, part):
        act_copy(slot, slot, part, z_send.at[0, 0], sibling).wait_recv()

    to_up = lambda part: act_copy(0, 3, part, z_send.at[0, part], z_up)
    to_down = lambda part: act_copy(0, 2, part, z_send.at[1, part], z_down)
    on_up = lambda: act_copy(3, 6, 0, z_send.at[2, 0], z_up)
    on_down = lambda: act_copy(2, 6, 1, z_send.at[2, 1], z_down)
    y_slot = {0: 1, 2: 4, 3: 5, 6: 7}
    to_mate = lambda slot, part: act_copy(slot, y_slot[slot], part, y_send.at[slot, part], y_mate)

    w_own = pltpu.make_async_copy(w_ref, weights.at[0], w_sem)
    w_own.start()
    w_pair = remote(w_ref, weights.at[1], w_send, w_recv, y_pair)
    w_pair.start()
    acts[0] = own_ref[...]
    to_up(0).start()
    to_down(1).start()
    to_mate(0, 0).start()
    to_up(1).start()
    to_down(0).start()
    to_mate(0, 1).start()

    def split(step):
        slot = jnp.where(step < 7, step, jnp.where(step < 14, step - 7, 7))
        w = jnp.where(step < 7, 0, jnp.where(step < 14, 1, step - 14))
        ahead = jnp.where(slot < 2, 0, jnp.where(slot < 6, 1 + 2 * (slot % 2), 2))
        group = jnp.where(slot < 2, slot, jnp.where(slot < 6, (slot - 2) // 2, slot - 6))
        away = (x + 8 - zh - ahead) % 4
        return slot, w, group, away

    def leaf_copies(step, which):
        return (
            remote(
                tree_out.at[step, pl.ds(0, rows)], leaf_in.at[which, 1],
                leaf_send.at[which, 0], leaf_recv.at[which, 1], x_up,
            ),
            remote(
                tree_out.at[step, pl.ds(rows, rows)], leaf_in.at[which, 0],
                leaf_send.at[which, 1], leaf_recv.at[which, 0], x_down,
            ),
        )

    def root_copy(step, which, side):
        where = device(zh, y, (x + 3 + 2 * side) % 4, zl, core)
        return remote(
            tree_out.at[step], root_in.at[which, side], root_send.at[which, side],
            root_recv.at[which, side], where,
        )

    def last_copy(w, group, which):
        row = jnp.where(group == 0, y, mate)
        column = jnp.where(w == 0, y, pair)
        here = (w == 0) & (row // 2 == zl) & (row % 2 == core)
        copy = remote(
            last_out.at[which], last_in.at[zl * 2 + core], last_send.at[which],
            last_recv.at[zl * 2 + core], device(zh, column, x, row // 2, row % 2),
        )
        return here, copy

    def sib_copy(step):
        return remote(
            sib_out.at[step], sib_in.at[step], sib_send.at[step], sib_recv.at[step], sibling
        )

    def columns(part, tile):
        return pl.ds(pl.multiple_of(part * half + tile * 256, 256), 256)

    def product(slot, w, part, tile):
        return jnp.dot(
            acts[slot], weights[w, :, columns(part, tile)], preferred_element_type=jnp.float32
        )

    def tick(step, carry):
        @pl.when(step == 1)
        def _():
            act_wait(3, 0)
            on_up().start()
            to_mate(3, 0).start()
            act_wait(2, 1)
            on_down().start()
            to_mate(2, 1).start()

        @pl.when(step == 2)
        def _():
            act_wait(2, 0)
            to_mate(2, 0).start()
            act_wait(3, 1)
            to_mate(3, 1).start()

        @pl.when(step == 4)
        def _():
            for part in range(2):
                act_wait(6, part)
                to_mate(6, part).start()

        @pl.when((step == 1) | (step == 4) | (step == 5) | (step == 14))
        def _():
            slot = jnp.where(step == 14, 7, step)
            act_wait(slot, 0)
            act_wait(slot, 1)

        @pl.when(step == 0)
        def _():
            w_own.wait()

        @pl.when(step == 7)
        def _():
            w_pair.wait_recv()

        @pl.when(step < 16)
        def _():
            slot, w, _, _ = split(step)

            def give(tile, c):
                sib_out[step, :, pl.ds(pl.multiple_of(tile * 256, 256), 256)] = product(
                    slot, w, 1 - core, tile
                ).astype(jnp.bfloat16)
                return c

            lax.fori_loop(0, tiles, give, 0)
            sib_copy(step).start()

            def keep(tile, c):
                held[step % 4, :, pl.ds(pl.multiple_of(tile * 256, 256), 256)] = product(
                    slot, w, core, tile
                )
                return c

            lax.fori_loop(0, tiles, keep, 0)

        @pl.when((step >= 1) & (step < 17))
        def _():
            old = step - 1
            _, w, group, away = split(old)
            which = group * 2 + w

            @pl.when(away % 2 == 1)
            def _():
                side = away // 2
                first = pl.multiple_of((1 - side) * rows, rows)
                remote(
                    leaf_in.at[which, side], leaf_in.at[which, side], leaf_send.at[which, 0],
                    leaf_recv.at[which, side], sibling,
                ).wait_recv()
                tree_out[old, pl.ds(first, rows)] = (
                    held[old % 4, pl.ds(first, rows)] + leaf_in[which, side].astype(jnp.float32)
                ).astype(jnp.bfloat16)
                other = pl.multiple_of(side * rows, rows)
                tree_out[old, pl.ds(other, rows)] = held[old % 4, pl.ds(other, rows)].astype(
                    jnp.bfloat16
                )
                root_copy(old, which, side).start()

        @pl.when(step >= 2)
        def _():
            old = step - 2
            _, w, group, away = split(old)
            which = group * 2 + w

            @pl.when(away == 0)
            def _():
                for side in range(2):
                    root_copy(old, which, side).wait_recv()
                last_out[which] = (
                    held[old % 4]
                    + root_in[which, 0].astype(jnp.float32)
                    + root_in[which, 1].astype(jnp.float32)
                ).astype(jnp.bfloat16)
                here, copy = last_copy(w, group, which)

                @pl.when(here)
                def _():
                    last_in[zl * 2 + core] = last_out[which]

                @pl.when(jnp.logical_not(here))
                def _():
                    copy.start()

        @pl.when(step < 16)
        def _():
            _, w, group, away = split(step)
            which = group * 2 + w
            sib_copy(step).wait_recv()

            @pl.when(away == 2)
            def _():
                tree_out[step] = (held[step % 4] + sib_in[step].astype(jnp.float32)).astype(
                    jnp.bfloat16
                )
                for copy in leaf_copies(step, which):
                    copy.start()

            @pl.when(away != 2)
            def _():
                held[step % 4] = held[step % 4] + sib_in[step].astype(jnp.float32)

        return carry

    lax.fori_loop(0, 18, tick, 0)

    for zs in range(2):
        for cs in range(2):
            @pl.when((near == 0) | (zs != zl) | (cs != core))
            def _():
                remote(
                    last_in.at[zs * 2 + cs], last_in.at[zs * 2 + cs], last_send.at[0],
                    last_recv.at[zs * 2 + cs], sibling,
                ).wait_recv()
    for cs in range(2):
        out_ref[:, cs * half:(cs + 1) * half] = (
            last_in[cs].astype(jnp.float32) + last_in[2 + cs].astype(jnp.float32)
        ).astype(jnp.bfloat16)

    w_pair.wait_send()
    for part in range(2):
        to_up(part).wait_send()
        to_down(part).wait_send()
        for slot in y_slot:
            to_mate(slot, part).wait_send()
    on_up().wait_send()
    on_down().wait_send()

    def drain(step, carry):
        _, w, group, away = split(step)
        which = group * 2 + w
        sib_copy(step).wait_send()

        @pl.when(away == 2)
        def _():
            for copy in leaf_copies(step, which):
                copy.wait_send()

        @pl.when(away % 2 == 1)
        def _():
            root_copy(step, which, away // 2).wait_send()

        @pl.when(away == 0)
        def _():
            here, copy = last_copy(w, group, which)

            @pl.when(jnp.logical_not(here))
            def _():
                copy.wait_send()

        return carry

    lax.fori_loop(0, 16, drain, 0)


def project(head_out, out_weight):
    tokens, depth = head_out.shape
    width = out_weight.shape[1]
    half = width // 2
    bf16 = jnp.bfloat16
    dma = pltpu.SemaphoreType.DMA
    return pl.pallas_call(
        project_kernel,
        out_shape=jax.ShapeDtypeStruct((tokens, width), bf16),
        in_specs=[pl.BlockSpec(memory_space=pltpu.VMEM), pl.BlockSpec(memory_space=pl.ANY)],
        out_specs=pl.BlockSpec(memory_space=pltpu.VMEM),
        scratch_shapes=[
            pltpu.VMEM((8, tokens, depth), bf16),
            pltpu.VMEM((2, depth, width), bf16),
            pltpu.VMEM((16, tokens, half), bf16),
            pltpu.VMEM((16, tokens, half), bf16),
            pltpu.VMEM((4, tokens, half), jnp.float32),
            pltpu.VMEM((16, tokens, half), bf16),
            pltpu.VMEM((4, 2, tokens // 2, half), bf16),
            pltpu.VMEM((4, 2, tokens, half), bf16),
            pltpu.VMEM((4, tokens, half), bf16),
            pltpu.VMEM((4, tokens, half), bf16),
            dma, dma, dma,
            dma((8, 2)), dma((3, 2)), dma((8, 2)), dma((16,)), dma((16,)),
            dma((4, 2)), dma((4, 2)), dma((4, 2)), dma((4, 2)), dma((4,)), dma((4,)),
        ],
        compiler_params=pltpu.CompilerParams(
            collective_id=0, has_side_effects=True, vmem_limit_bytes=56 * 1024 * 1024
        ),
    )(head_out, out_weight)


def rotate_heads(states, positions):
    half_width = states.shape[-1] // 2
    exponents = jnp.arange(half_width, dtype=jnp.float32) * (2.0 / states.shape[-1])
    inverse_freq = 500000.0 ** (-exponents)
    angles = positions.astype(jnp.float32)[:, None] * inverse_freq[None, :]
    cosine = jnp.cos(angles)[:, None, :]
    sine_part = jnp.sin(angles)[:, None, :]
    front_half = states[..., :half_width]
    back_half = states[..., half_width:]
    return jnp.concatenate(
        [front_half * cosine - back_half * sine_part, back_half * cosine + front_half * sine_part],
        axis=-1,
    )


def per_device(
    queries, key_states, value_states, vertical_blocks, slash_offsets, positions, out_weight
):
    local_tokens = queries.shape[0]
    local_heads = queries.shape[1] // HD
    head_index = lax.axis_index("head")
    ctx_index = lax.axis_index("ctx")
    shared_head = head_index * local_heads // GROUP
    own_keys = lax.dynamic_slice_in_dim(key_states, shared_head * HD, HD, 1)
    own_values = lax.dynamic_slice_in_dim(value_states, shared_head * HD, HD, 1)
    rotated_own = rotate_heads(own_keys.astype(jnp.float32)[:, None, :], positions)[:, 0, :].astype(
        jnp.bfloat16
    )
    all_keys, all_values = (
        lax.all_gather(rotated_own, "ctx", axis=0, tiled=True),
        lax.all_gather(own_values, "ctx", axis=0, tiled=True),
    )
    query_rot = rotate_heads(
        queries.astype(jnp.float32).reshape(local_tokens, local_heads, HD), positions
    ).astype(jnp.bfloat16)
    query_blocks = local_tokens // BLK
    key_count = all_keys.shape[0] // BLK
    block_ids = ctx_index * query_blocks + jnp.arange(query_blocks, dtype=jnp.int32)
    vert_slots = jnp.broadcast_to(
        vertical_blocks[:, None, :], (local_heads, query_blocks, vertical_blocks.shape[1])
    )
    vert_valid = vert_slots <= block_ids[None, :, None]
    slash_slots = block_ids[None, :, None] - slash_offsets[:, None, :]
    repeated = jnp.any(slash_slots[..., None] == vertical_blocks[:, None, None, :], axis=-1)
    slash_valid = (slash_slots >= 0) & jnp.logical_not(repeated)
    slot_blocks = jnp.concatenate([vert_slots, slash_slots], axis=-1)
    slot_valid = jnp.concatenate([vert_valid, slash_valid], axis=-1)
    safe_blocks = jnp.clip(slot_blocks, 0, key_count - 1)
    key_tiles = all_keys.reshape(key_count, BLK, HD)[safe_blocks]
    value_tiles = all_values.reshape(key_count, BLK, HD)[safe_blocks]
    query_tiles = query_rot.reshape(query_blocks, BLK, local_heads, HD).transpose(2, 0, 1, 3)
    scores = jnp.einsum(
        "hqrd,hqskd->hqrsk", query_tiles, key_tiles, preferred_element_type=jnp.float32
    ) / math.sqrt(HD)
    diagonal = (slot_blocks == block_ids[None, :, None])[:, :, None, :, None]
    causal_pairs = (jnp.arange(BLK)[None, :] <= jnp.arange(BLK)[:, None])[None, None, :, None, :]
    allowed = slot_valid[:, :, None, :, None] & (jnp.logical_not(diagonal) | causal_pairs)
    masked = jnp.where(allowed, scores, -1e30)
    row_max = jnp.max(masked, axis=(3, 4), keepdims=True)
    exponentials = jnp.exp(masked - row_max)
    weights = (exponentials / jnp.sum(exponentials, axis=(3, 4), keepdims=True)).astype(
        jnp.bfloat16
    )
    attended = jnp.einsum(
        "hqrsk,hqskd->hqrd", weights, value_tiles, preferred_element_type=jnp.float32
    ).astype(jnp.bfloat16)
    head_out = attended.transpose(1, 2, 0, 3).reshape(local_tokens, local_heads * HD)
    return project(head_out, out_weight)


def solution(mesh):
    placed = (
        P("ctx", "head"),
        P("ctx", None),
        P("ctx", None),
        P("head", None),
        P("head", None),
        P("ctx"),
        P("head", "ctx"),
    )
    return jax.shard_map(
        per_device, mesh=mesh, in_specs=placed, out_specs=P("head", "ctx"), check_vma=False
    )
```

```python
import math

import jax
import jax.numpy as jnp
from jax import lax
from jax.experimental import pallas as pl
from jax.experimental.pallas import tpu as pltpu
from jax.sharding import PartitionSpec as P

HD = 128
BLK = 128
MESH = pl.DeviceIdType.MESH
BF16 = jnp.bfloat16
F32 = jnp.float32

ORDER = (0, -1, -1, 1, -1, -1, 2, 3, 8, 9, 4, 5, 6, 10, 11, 12, 13, 14, 7, 15)
HOP2, HOP3, HOP4 = 2, 4, 6


def place():
    ctx = lax.axis_index("ctx")
    head = lax.axis_index("head")
    return ctx // 4, ctx % 4, head // 4, (head // 2) % 2, head % 2


def device(zh, y, x, zl, core):
    return {"ctx": (zh % 4) * 4 + y % 4, "head": (x % 4) * 4 + zl * 2 + core}


def remote(src, dst, send, recv, where):
    return pltpu.make_async_remote_copy(
        src_ref=src, dst_ref=dst, send_sem=send, recv_sem=recv, device_id=where, device_id_type=MESH
    )


def turned(states, cosine, sine):
    states = states.astype(F32)
    return (states * cosine + pltpu.roll(states, HD // 2, 1) * sine).astype(BF16)


def kernel(
    vert_ref, slash_ref, q_ref, cos_ref, sin_ref, k_ref, v_ref, w_ref, out_ref,
    k_own, v_own, q_rot, kv, acts, weights, sib_out, sib_in, held, chain_out, chain_in,
    last_out, last_in,
    own_sem, w_sem, w_send, w_recv, kz_send, kz_recv, ky_send, ky_recv, ks_send, ks_recv,
    act_recv, z_send, y_send, sib_send, sib_recv, chain_send, chain_recv, last_send, last_recv,
):
    zh, y, x, zl, core = place()
    mate = 3 - y
    pair = y + 1 - 2 * (y % 2)
    z_up = device(zh + 1, y, x, zl, core)
    z_down = device(zh + 3, y, x, zl, core)
    y_up = device(zh, y + 1, x, zl, core)
    y_down = device(zh, y + 3, x, zl, core)
    y_mate = device(zh, mate, x, zl, core)
    y_pair = device(zh, pair, x, zl, core)
    x_up = device(zh, y, x + 1, zl, core)
    x_down = device(zh, y, x + 3, zl, core)
    sibling = device(zh, y, x, zl, 1 - core)
    half = sib_out.shape[2]
    rows = acts.shape[1] // 2
    tiles = half // 256
    heads = q_ref.shape[1] // HD

    kv_column = pl.multiple_of((x * 2 + zl) * HD, HD)
    own_rows = pl.ds(pl.multiple_of(core * BLK, BLK), BLK)
    k_copy = pltpu.make_async_copy(
        k_ref.at[own_rows, pl.ds(kv_column, HD)], k_own, own_sem.at[0]
    )
    v_copy = pltpu.make_async_copy(
        v_ref.at[own_rows, pl.ds(kv_column, HD)], v_own, own_sem.at[1]
    )
    w_own = pltpu.make_async_copy(w_ref, weights.at[0], w_sem)
    k_copy.start()
    v_copy.start()
    w_own.start()

    token_row = zl * 2 + core
    near = jnp.where((token_row == y) | (token_row == mate), 1, 0)
    source_row = jnp.where(near == 1, y, pair)

    barrier = pltpu.get_barrier_semaphore()

    def greet(where):
        pl.semaphore_signal(barrier, inc=1, device_id=where, device_id_type=MESH)

    for where in (z_up, z_down, y_up, y_down, x_up, x_down, sibling):
        greet(where)
    for zs in range(2):
        for cs in range(2):
            @pl.when((near == 0) | (zs != zl) | (cs != core))
            def _():
                greet(device(zh, source_row, x, zs, cs))

    def block(dz, dy, which=core):
        return (((zh + dz) % 4) * 4 + (y + dy) % 4) * 2 + which

    mine = block(0, 0)
    k_copy.wait()
    v_copy.wait()
    kv[mine, 0] = turned(k_own[...], cos_ref[own_rows, :], sin_ref[own_rows, :])
    kv[mine, 1] = v_own[...].astype(F32).T.astype(BF16)
    pl.semaphore_wait(barrier, 11 - near)

    def kz_copy(dz_there, index, where):
        return remote(kv.at[mine], kv.at[mine], kz_send.at[index], kz_recv.at[dz_there], where)

    def kz_on(dz, part, where):
        here = kv.at[block(dz, 0), part]
        return remote(here, here, kz_send.at[2 + part], kz_recv.at[2 + part], where)

    def ky_copy(dz, dy, index, there, where):
        here = kv.at[block(dz, dy)]
        return remote(here, here, ky_send.at[dz, index], ky_recv.at[dz, there], where)

    def ks_copy(dz, dy):
        here = kv.at[block(dz, dy)]
        return remote(here, here, ks_send.at[dz, dy], ks_recv.at[dz, dy], sibling)

    def kv_row(dz):
        return (ky_copy(dz, 0, 0, 3, y_up), ky_copy(dz, 0, 1, 1, y_down), ks_copy(dz, 0))

    def kv_far(dz):
        if dz < 2:
            return ky_copy(dz, 3, 2, 2, y_up)
        return ky_copy(dz, 1, 2, 2, y_down)

    kz_sends = (kz_copy(1, 0, z_up), kz_copy(0, 1, z_down), kz_on(3, 0, z_up), kz_on(1, 1, z_down))
    kz_sends[0].start()
    kz_sends[1].start()
    for copy in kv_row(0):
        copy.start()

    for h in range(heads):
        column = slice(h * HD, (h + 1) * HD)
        q_rot[:, column] = turned(q_ref[:, column], cos_ref[...], sin_ref[...])

    kz_sends[1].wait_recv()
    kz_sends[3].start()
    for copy in kv_row(1):
        copy.start()
    kz_sends[0].wait_recv()
    kz_sends[2].start()
    for copy in kv_row(3):
        copy.start()

    def kv_near(dz):
        for dy in (3, 1):
            ky_copy(dz, dy, 0, dy, sibling).wait_recv()
            if (dy == 3) == (dz < 2):
                kv_far(dz).start()
            ks_copy(dz, dy).start()

    kv_near(0)
    kz_sends[2].wait_recv()
    kz_sends[3].wait_recv()
    for copy in kv_row(2):
        copy.start()
    kv_near(1)
    kv_near(3)
    w_pair = remote(w_ref, weights.at[1], w_send, w_recv, y_pair)
    w_pair.start()
    kv_near(2)
    for dz in range(4):
        ky_copy(dz, 2, 0, 2, sibling).wait_recv()
        ks_copy(dz, 2).start()
    for dz in range(4):
        for dy in range(4):
            ks_copy(dz, dy).wait_recv()

    def act_copy(src_slot, dst_slot, part, send, where):
        return remote(
            acts.at[src_slot, pl.ds(part * rows, rows)], acts.at[dst_slot, pl.ds(part * rows, rows)],
            send, act_recv.at[dst_slot, part], where,
        )

    def act_wait(slot, part):
        act_copy(slot, slot, part, z_send.at[0, 0], sibling).wait_recv()

    to_up = lambda part: act_copy(0, 3, part, z_send.at[0, part], z_up)
    to_down = lambda part: act_copy(0, 2, part, z_send.at[1, part], z_down)
    on_up = lambda: act_copy(3, 6, 0, z_send.at[2, 0], z_up)
    on_down = lambda: act_copy(2, 6, 1, z_send.at[2, 1], z_down)
    y_slot = {0: 1, 2: 4, 3: 5, 6: 7}
    to_mate = lambda slot, part: act_copy(slot, y_slot[slot], part, y_send.at[slot, part], y_mate)

    scale = math.log2(math.e) / math.sqrt(HD)
    ctx = zh * 4 + y

    def attend(part):
        here = ctx * 2 + part

        def one_head(h, carry):
            column = pl.ds(pl.multiple_of(h * HD, HD), HD)
            query = q_rot[part * BLK:(part + 1) * BLK, column]
            vertical = [vert_ref[h, s] for s in range(4)]
            blocks = [here] + vertical
            bias = [None] + [jnp.where(b < here, 0.0, -1e30) for b in vertical]
            for s in range(1, 4):
                b = here - slash_ref[h, s]
                seen = (b == vertical[0]) | (b == vertical[1]) | (b == vertical[2]) | (b == vertical[3])
                blocks.append(jnp.maximum(b, 0))
                bias.append(jnp.where((b >= 0) & jnp.logical_not(seen), 0.0, -1e30))
            keys = jnp.concatenate([kv[b, 0] for b in blocks], axis=0)
            values = jnp.concatenate([kv[b, 1] for b in blocks], axis=1)
            scores = lax.dot_general(
                keys, query, (((1,), (1,)), ((), ())), preferred_element_type=F32
            ) * scale
            tiles_of = [scores[s * BLK:(s + 1) * BLK] for s in range(8)]
            key_row = lax.broadcasted_iota(jnp.int32, (BLK, BLK), 0)
            query_row = lax.broadcasted_iota(jnp.int32, (BLK, BLK), 1)
            tiles_of[0] = jnp.where(key_row <= query_row, tiles_of[0], -1e30)
            top = jnp.max(tiles_of[0], axis=0, keepdims=True)
            for s in range(1, 8):
                top = jnp.maximum(top, jnp.max(tiles_of[s], axis=0, keepdims=True) + bias[s])
            powers = [jnp.exp2(tiles_of[0] - top)]
            for s in range(1, 8):
                powers.append(jnp.exp2(tiles_of[s] - (top - bias[s])))
            total = sum(jnp.sum(p, axis=0, keepdims=True) for p in powers)
            mixed = jnp.dot(
                values, jnp.concatenate([p.astype(BF16) for p in powers], axis=0),
                preferred_element_type=F32,
            )
            acts[0, part * BLK:(part + 1) * BLK, column] = (mixed * (1.0 / total)).T.astype(BF16)
            return carry

        lax.fori_loop(0, heads, one_head, 0)

    for part in range(2):
        attend(part)
        to_up(part).start()
        to_down(part).start()
        to_mate(0, part).start()

    def split(step):
        slot = step % 8
        ahead = jnp.where(slot < 2, 0, jnp.where(slot < 6, 1 + 2 * (slot % 2), 2))
        group = jnp.where(slot < 2, slot, jnp.where(slot < 6, (slot - 2) // 2, slot - 6))
        return slot, step // 8, group, (x + 8 - zh - ahead) % 4

    def chain_copy(step, part):
        here = pl.ds(part * rows, rows)
        return remote(
            chain_out.at[step, here], chain_in.at[step, here], chain_send.at[step, part],
            chain_recv.at[step, part], x_down if part else x_up,
        )

    def last_copy(w, group):
        which = group * 2 + w
        row = jnp.where(group == 0, y, mate)
        column = jnp.where(w == 0, y, pair)
        here = (w == 0) & (row // 2 == zl) & (row % 2 == core)
        copy = remote(
            last_out.at[which], last_in.at[zl * 2 + core], last_send.at[which],
            last_recv.at[zl * 2 + core], device(zh, column, x, row // 2, row % 2),
        )
        return here, copy

    def sib_copy(step):
        return remote(
            sib_out.at[step], sib_in.at[step], sib_send.at[step], sib_recv.at[step], sibling
        )

    def product(slot, w, side, tile):
        column = pl.ds(pl.multiple_of(side * half + tile * 256, 256), 256)
        return jnp.dot(acts[slot], weights[w, :, column], preferred_element_type=F32)

    def pass_on(step, spot, part):
        here = slice(part * rows, (part + 1) * rows)
        chain_copy(step, part).wait_recv()
        chain_out[step, here] = (held[spot, here] + chain_in[step, here].astype(F32)).astype(BF16)
        chain_copy(step, part).start()

    def work_at(position):
        step = jnp.int32(-1)
        for spot, entry in enumerate(ORDER):
            if entry >= 0:
                step = jnp.where(position == spot, entry, step)
        return step

    def tick(position, carry):
        step = work_at(position)
        slot, w, group, away = split(jnp.maximum(step, 0))
        spot = position % 8

        @pl.when(step == 1)
        def _():
            act_wait(3, 0)
            on_up().start()
            to_mate(3, 0).start()
            act_wait(2, 0)
            to_mate(2, 0).start()

        @pl.when(step == 2)
        def _():
            act_wait(2, 1)
            on_down().start()
            to_mate(2, 1).start()
            act_wait(3, 1)
            to_mate(3, 1).start()

        @pl.when(step == 4)
        def _():
            for part in range(2):
                act_wait(6, part)
                to_mate(6, part).start()

        @pl.when((step == 1) | (step == 4) | (step == 5) | (step == 7))
        def _():
            act_wait(slot, 0)
            act_wait(slot, 1)

        @pl.when(step == 0)
        def _():
            w_own.wait()

        @pl.when(step == 8)
        def _():
            w_pair.wait_recv()

        @pl.when(step >= 0)
        def _():
            def give(tile, c):
                sib_out[step, :, pl.ds(pl.multiple_of(tile * 256, 256), 256)] = product(
                    slot, w, 1 - core, tile
                ).astype(BF16)
                return c

            lax.fori_loop(0, tiles, give, 0)
            sib_copy(step).start()

            def keep(tile, c):
                held[spot, :, pl.ds(pl.multiple_of(tile * 256, 256), 256)] = product(
                    slot, w, core, tile
                )
                return c

            lax.fori_loop(0, tiles, keep, 0)

        two = work_at(position - HOP2)
        away_two = split(jnp.maximum(two, 0))[3]

        @pl.when((two >= 0) & (away_two == 2))
        def _():
            for part in range(2):
                pass_on(two, (position + 8 - HOP2) % 8, part)

        three = work_at(position - HOP3)
        away_three = split(jnp.maximum(three, 0))[3]

        @pl.when((three >= 0) & (away_three == 3))
        def _():
            pass_on(three, (position + 8 - HOP3) % 8, 0)

        @pl.when((three >= 0) & (away_three == 1))
        def _():
            pass_on(three, (position + 8 - HOP3) % 8, 1)

        four = work_at(position - HOP4)
        _, w_four, group_four, away_four = split(jnp.maximum(four, 0))

        @pl.when((four >= 0) & (away_four == 0))
        def _():
            which = group_four * 2 + w_four
            for part in range(2):
                chain_copy(four, part).wait_recv()
            last_out[which] = (
                held[(position + 8 - HOP4) % 8] + chain_in[four].astype(F32)
            ).astype(BF16)
            here, copy = last_copy(w_four, group_four)

            @pl.when(here)
            def _():
                last_in[zl * 2 + core] = last_out[which]

            @pl.when(jnp.logical_not(here))
            def _():
                copy.start()

        @pl.when(step >= 0)
        def _():
            sib_copy(step).wait_recv()
            held[spot] = held[spot] + sib_in[step].astype(F32)

            @pl.when(away == 1)
            def _():
                chain_out[step, 0:rows] = held[spot, 0:rows].astype(BF16)
                chain_copy(step, 0).start()

            @pl.when(away == 3)
            def _():
                chain_out[step, rows:] = held[spot, rows:].astype(BF16)
                chain_copy(step, 1).start()

        return carry

    lax.fori_loop(0, len(ORDER) + HOP4, tick, 0)

    for zs in range(2):
        for cs in range(2):
            @pl.when((near == 0) | (zs != zl) | (cs != core))
            def _():
                remote(
                    last_in.at[zs * 2 + cs], last_in.at[zs * 2 + cs], last_send.at[0],
                    last_recv.at[zs * 2 + cs], sibling,
                ).wait_recv()
    for cs in range(2):
        out_ref[:, cs * half:(cs + 1) * half] = (
            last_in[cs].astype(F32) + last_in[2 + cs].astype(F32)
        ).astype(BF16)

    w_pair.wait_send()
    for copy in kz_sends:
        copy.wait_send()
    for dz in range(4):
        for copy in kv_row(dz)[:2] + (kv_far(dz),):
            copy.wait_send()
        for dy in range(4):
            ks_copy(dz, dy).wait_send()
    for part in range(2):
        to_up(part).wait_send()
        to_down(part).wait_send()
        for slot in y_slot:
            to_mate(slot, part).wait_send()
    on_up().wait_send()
    on_down().wait_send()

    def drain(step, carry):
        _, w, group, away = split(step)
        sib_copy(step).wait_send()

        @pl.when(away != 0)
        def _():
            for part in range(2):
                chain_copy(step, part).wait_send()

        @pl.when(away == 0)
        def _():
            here, copy = last_copy(w, group)

            @pl.when(jnp.logical_not(here))
            def _():
                copy.wait_send()

        return carry

    lax.fori_loop(0, 16, drain, 0)


def per_device(
    queries, key_states, value_states, vertical_blocks, slash_offsets, positions, out_weight
):
    tokens, depth = queries.shape
    width = out_weight.shape[1]
    half = width // 2
    exponents = jnp.arange(HD // 2, dtype=F32) * (2.0 / HD)
    inverse_freq = 500000.0 ** (-exponents)
    angles = positions.astype(F32)[:, None] * inverse_freq[None, :]
    cosine = jnp.cos(angles)
    sine = jnp.sin(angles)
    cosine = jnp.concatenate([cosine, cosine], axis=1)
    sine = jnp.concatenate([-sine, sine], axis=1)
    vmem = pl.BlockSpec(memory_space=pltpu.VMEM)
    smem = pl.BlockSpec(memory_space=pltpu.SMEM)
    anywhere = pl.BlockSpec(memory_space=pl.ANY)
    dma = pltpu.SemaphoreType.DMA
    return pl.pallas_call(
        kernel,
        out_shape=jax.ShapeDtypeStruct((tokens, width), BF16),
        in_specs=[smem, smem, vmem, vmem, vmem, anywhere, anywhere, anywhere],
        out_specs=vmem,
        scratch_shapes=[
            pltpu.VMEM((BLK, HD), BF16),
            pltpu.VMEM((BLK, HD), BF16),
            pltpu.VMEM((tokens, depth), BF16),
            pltpu.VMEM((32, 2, BLK, HD), BF16),
            pltpu.VMEM((8, tokens, depth), BF16),
            pltpu.VMEM((2, depth, width), BF16),
            pltpu.VMEM((16, tokens, half), BF16),
            pltpu.VMEM((16, tokens, half), BF16),
            pltpu.VMEM((8, tokens, half), F32),
            pltpu.VMEM((16, tokens, half), BF16),
            pltpu.VMEM((16, tokens, half), BF16),
            pltpu.VMEM((4, tokens, half), BF16),
            pltpu.VMEM((4, tokens, half), BF16),
            dma((2,)), dma, dma, dma,
            dma((4,)), dma((4,)), dma((4, 3)), dma((4, 4)), dma((4, 4)), dma((4, 4)),
            dma((8, 2)), dma((3, 2)), dma((8, 2)), dma((16,)), dma((16,)),
            dma((16, 2)), dma((16, 2)), dma((4,)), dma((4,)),
        ],
        compiler_params=pltpu.CompilerParams(
            collective_id=0, has_side_effects=True, vmem_limit_bytes=56 * 1024 * 1024
        ),
    )(
        vertical_blocks, slash_offsets, queries, cosine, sine, key_states, value_states, out_weight
    )


def solution(mesh):
    placed = (
        P("ctx", "head"),
        P("ctx", None),
        P("ctx", None),
        P("head", None),
        P("head", None),
        P("ctx"),
        P("head", "ctx"),
    )
    return jax.shard_map(
        per_device, mesh=mesh, in_specs=placed, out_specs=P("head", "ctx"), check_vma=False
    )
```

```python
import math

import jax
import jax.numpy as jnp
import numpy as np
from jax import lax
from jax.experimental import pallas as pl
from jax.experimental.pallas import tpu as pltpu
from jax.sharding import PartitionSpec as P

HD = 128
BLK = 128
MESH = pl.DeviceIdType.MESH
BF16 = jnp.bfloat16
F32 = jnp.float32

ORDER = (0, -1, -1, 1, -1, -1, 2, 3, 8, 9, 4, 5, 6, 10, 11, 12, 13, 14, 7, 15)
HOP2, HOP3, HOP4 = 3, 6, 9


def place():
    ctx = lax.axis_index("ctx")
    head = lax.axis_index("head")
    return ctx // 4, ctx % 4, head // 4, (head // 2) % 2, head % 2


def device(zh, y, x, zl, core):
    return {"ctx": (zh % 4) * 4 + y % 4, "head": (x % 4) * 4 + zl * 2 + core}


def remote(src, dst, send, recv, where):
    return pltpu.make_async_remote_copy(
        src_ref=src, dst_ref=dst, send_sem=send, recv_sem=recv, device_id=where, device_id_type=MESH
    )


def turned(states, cosine, sine):
    states = states.astype(F32)
    return states * cosine + pltpu.roll(states, HD // 2, 1) * sine


def kernel(
    vert_in, slash_in, pos_in, freq_ref, q_in, k_ref, v_ref, w_ref, last_in,
    vert_ref, slash_ref, pos_ref, q_ref, k_own, v_own, q_rot, kv, acts, weights, held, chain_out,
    chain_in, last_out,
    own_sem, w_sem, w_send, w_recv, kz_send, kz_recv, ky_send, ky_recv, ks_send, ks_recv,
    act_recv, as_send, as_recv, z_send, y_send, chain_send, chain_recv, last_send, last_recv,
):
    zh, y, x, zl, core = place()
    mate = 3 - y
    pair = y + 1 - 2 * (y % 2)
    z_up = device(zh + 1, y, x, zl, core)
    z_down = device(zh + 3, y, x, zl, core)
    y_up = device(zh, y + 1, x, zl, core)
    y_down = device(zh, y + 3, x, zl, core)
    y_mate = device(zh, mate, x, zl, core)
    y_pair = device(zh, pair, x, zl, core)
    y_pair_sibling = device(zh, pair, x, zl, 1 - core)
    x_up = device(zh, y, x + 1, zl, core)
    x_down = device(zh, y, x + 3, zl, core)
    sibling = device(zh, y, x, zl, 1 - core)
    half = weights.shape[2]
    depth = q_ref.shape[1]
    rows = acts.shape[1] // 2
    tiles = half // 256
    heads = q_ref.shape[1] // HD

    kv_column = pl.multiple_of((x * 2 + zl) * HD, HD)
    own_rows = pl.ds(pl.multiple_of(core * BLK, BLK), BLK)
    small = [
        pltpu.make_async_copy(src, dst, own_sem.at[i])
        for i, (src, dst) in enumerate((
            (pos_in, pos_ref),
            (k_ref.at[own_rows, pl.ds(kv_column, HD)], k_own),
            (v_ref.at[own_rows, pl.ds(kv_column, HD)], v_own),
            (q_in, q_ref),
            (vert_in, vert_ref),
            (slash_in, slash_ref),
        ))
    ]
    for copy in small:
        copy.start()

    depth_here = pl.ds(pl.multiple_of(core * depth, depth), depth)

    def w_part(which):
        return w_ref.at[:, pl.ds(pl.multiple_of(which * half, half), half)]

    w_own = pltpu.make_async_copy(w_part(core), weights.at[0, depth_here], w_sem)
    w_others = [
        remote(w_part(which), weights.at[slot, depth_here], w_send.at[i], w_recv.at[i], where)
        for i, (which, slot, where) in enumerate((
            (1 - core, 0, sibling), (core, 1, y_pair), (1 - core, 1, y_pair_sibling),
        ))
    ]
    w_own.start()

    token_row = zl * 2 + core
    near = jnp.where((token_row == y) | (token_row == mate), 1, 0)
    source_row = jnp.where(near == 1, y, pair)

    barrier = pltpu.get_barrier_semaphore()

    def greet(where):
        pl.semaphore_signal(barrier, inc=1, device_id=where, device_id_type=MESH)

    for where in (z_up, z_down, y_up, y_down, x_up, x_down, sibling, y_pair_sibling):
        greet(where)
    for zs in range(2):
        for cs in range(2):
            @pl.when((near == 0) | (zs != zl) | (cs != core))
            def _():
                greet(device(zh, source_row, x, zs, cs))

    def block(dz, dy, which=core):
        return (((zh + dz) % 4) * 4 + (y + dy) % 4) * 2 + which

    mine = block(0, 0)
    small[0].wait()
    lane = lax.broadcasted_iota(jnp.int32, (BLK, HD), 1)
    row = lax.broadcasted_iota(jnp.int32, (BLK, HD), 0)
    first = lane < HD // 2
    start = jnp.where(first, pos_ref[0], pos_ref[BLK])
    angles = (start + row).astype(F32) * freq_ref[0:1, :]
    cosine = jnp.cos(angles)
    sine = jnp.sin(angles)
    cosine_other = pltpu.roll(cosine, HD // 2, 1)
    sine_other = pltpu.roll(sine, HD // 2, 1)
    tables = (
        (jnp.where(first, cosine, cosine_other), jnp.where(first, -sine, sine_other)),
        (jnp.where(first, cosine_other, cosine), jnp.where(first, -sine_other, sine)),
    )
    small[1].wait()
    small[2].wait()
    kv[mine, 0] = turned(
        k_own[...], *(jnp.where(core == 0, one, two) for one, two in zip(*tables))
    ).astype(BF16)
    kv[mine, 1] = v_own[...].astype(F32).T.astype(BF16)
    pl.semaphore_wait(barrier, 12 - near)

    def kz_copy(dz_there, index, where):
        return remote(kv.at[mine], kv.at[mine], kz_send.at[index], kz_recv.at[dz_there], where)

    def kz_on(dz, part, where):
        here = kv.at[block(dz, 0), part]
        return remote(here, here, kz_send.at[2 + part], kz_recv.at[2 + part], where)

    def ky_copy(dz, dy, index, there, where):
        here = kv.at[block(dz, dy)]
        return remote(here, here, ky_send.at[dz, index], ky_recv.at[dz, there], where)

    def ks_copy(dz, dy):
        here = kv.at[block(dz, dy)]
        return remote(here, here, ks_send.at[dz, dy], ks_recv.at[dz, dy], sibling)

    def kv_row(dz):
        return (ky_copy(dz, 0, 0, 3, y_up), ky_copy(dz, 0, 1, 1, y_down), ks_copy(dz, 0))

    def kv_far(dz):
        if dz < 2:
            return ky_copy(dz, 3, 2, 2, y_up)
        return ky_copy(dz, 1, 2, 2, y_down)

    kz_sends = (kz_copy(1, 0, z_up), kz_copy(0, 1, z_down), kz_on(3, 0, z_up), kz_on(1, 1, z_down))
    kz_sends[0].start()
    kz_sends[1].start()
    for copy in kv_row(0):
        copy.start()

    scale = math.log2(math.e) / math.sqrt(HD)
    small[3].wait()
    for part in range(2):
        cosine, sine = (table * scale for table in tables[part])
        for h in range(heads):
            states = q_ref[part * BLK:(part + 1) * BLK, h * HD:(h + 1) * HD]
            q_rot[part, h] = turned(states, cosine, sine).T.astype(BF16)
    small[4].wait()
    small[5].wait()

    kz_sends[1].wait_recv()
    kz_sends[3].start()
    for copy in kv_row(1):
        copy.start()
    kz_sends[0].wait_recv()
    kz_sends[2].start()
    for copy in kv_row(3):
        copy.start()

    def kv_near(dz):
        for dy in (3, 1):
            ky_copy(dz, dy, 0, dy, sibling).wait_recv()
            if (dy == 3) == (dz < 2):
                kv_far(dz).start()
            ks_copy(dz, dy).start()

    kv_near(0)
    kz_sends[2].wait_recv()
    kz_sends[3].wait_recv()
    for copy in kv_row(2):
        copy.start()
    kv_near(1)
    kv_near(3)
    kv_near(2)
    for copy in w_others:
        copy.start()
    for dz in range(4):
        ky_copy(dz, 2, 0, 2, sibling).wait_recv()
        ks_copy(dz, 2).start()
    for dz in range(4):
        for dy in range(4):
            ks_copy(dz, dy).wait_recv()

    def act_at(slot, part):
        return acts.at[slot, pl.ds(part * rows, rows), depth_here]

    def act_copy(src_slot, dst_slot, part, send, where):
        return remote(
            act_at(src_slot, part), act_at(dst_slot, part), send, act_recv.at[dst_slot, part], where
        )

    def share_copy(slot, part):
        here = act_at(slot, part)
        return remote(here, here, as_send.at[slot, part], as_recv.at[slot, part], sibling)

    def act_wait(slot, part):
        act_copy(slot, slot, part, z_send.at[0, 0], sibling).wait_recv()
        share_copy(slot, part).start()

    to_up = lambda part: act_copy(0, 3, part, z_send.at[0, part], z_up)
    to_down = lambda part: act_copy(0, 2, part, z_send.at[1, part], z_down)
    on_up = lambda: act_copy(3, 6, 0, z_send.at[2, 0], z_up)
    on_down = lambda: act_copy(2, 6, 1, z_send.at[2, 1], z_down)
    y_slot = {0: 1, 2: 4, 3: 5, 6: 7}
    to_mate = lambda slot, part: act_copy(slot, y_slot[slot], part, y_send.at[slot, part], y_mate)

    ctx = zh * 4 + y

    def attend(part):
        here = ctx * 2 + part

        def one_head(h, carry):
            column = pl.ds(pl.multiple_of(core * depth + h * HD, HD), HD)
            vertical = [vert_ref[s, h] for s in range(4)]
            blocks = [here] + vertical
            bias = [None] + [jnp.where(b < here, 0.0, -1e30) for b in vertical]
            for s in range(1, 4):
                b = here - slash_ref[s, h]
                seen = (b == vertical[0]) | (b == vertical[1]) | (b == vertical[2]) | (b == vertical[3])
                blocks.append(jnp.maximum(b, 0))
                bias.append(jnp.where((b >= 0) & jnp.logical_not(seen), 0.0, -1e30))
            keys = jnp.concatenate([kv[b, 0] for b in blocks], axis=0)
            values = jnp.concatenate([kv[b, 1] for b in blocks], axis=1)
            scores = jnp.dot(keys, q_rot[part, h], preferred_element_type=F32)
            tiles_of = [scores[s * BLK:(s + 1) * BLK] for s in range(8)]
            key_row = lax.broadcasted_iota(jnp.int32, (BLK, BLK), 0)
            query_row = lax.broadcasted_iota(jnp.int32, (BLK, BLK), 1)
            tiles_of[0] = jnp.where(key_row <= query_row, tiles_of[0], -1e30)
            top = jnp.max(tiles_of[0], axis=0, keepdims=True)
            for s in range(1, 8):
                top = jnp.maximum(top, jnp.max(tiles_of[s], axis=0, keepdims=True) + bias[s])
            powers = [jnp.exp2(tiles_of[0] - top)]
            for s in range(1, 8):
                powers.append(jnp.exp2(tiles_of[s] - (top - bias[s])))
            total = sum(jnp.sum(p, axis=0, keepdims=True) for p in powers)
            mixed = jnp.dot(
                values, jnp.concatenate([p.astype(BF16) for p in powers], axis=0),
                preferred_element_type=F32,
            )
            acts[0, part * BLK:(part + 1) * BLK, column] = (mixed * (1.0 / total)).T.astype(BF16)
            return carry

        lax.fori_loop(0, heads, one_head, 0)

    for part in range(2):
        attend(part)
        to_up(part).start()
        to_down(part).start()
        to_mate(0, part).start()
        share_copy(0, part).start()

    def split(step):
        slot = step % 8
        ahead = jnp.where(slot < 2, 0, jnp.where(slot < 6, 1 + 2 * (slot % 2), 2))
        group = jnp.where(slot < 2, slot, jnp.where(slot < 6, (slot - 2) // 2, slot - 6))
        return slot, step // 8, group, (x + 8 - zh - ahead) % 4

    def chain_copy(step, part):
        here = pl.ds(part * rows, rows)
        return remote(
            chain_out.at[step, here], chain_in.at[step, here], chain_send.at[step, part],
            chain_recv.at[step, part], x_down if part else x_up,
        )

    last_columns = pl.ds(pl.multiple_of(core * half, half), half)

    def last_copy(w, group):
        which = group * 2 + w
        row = jnp.where(group == 0, y, mate)
        column = jnp.where(w == 0, y, pair)
        here = (w == 0) & (row // 2 == zl) & (row % 2 == core)
        copy = remote(
            last_out.at[which], last_in.at[zl, :, last_columns], last_send.at[which],
            last_recv.at[zl * 2 + core], device(zh, column, x, row // 2, row % 2),
        )
        return here, copy

    def pass_on(step, spot, part):
        here = slice(part * rows, (part + 1) * rows)
        chain_copy(step, part).wait_recv()
        chain_out[step, here] = (held[spot, here] + chain_in[step, here].astype(F32)).astype(BF16)
        chain_copy(step, part).start()

    def work_at(position):
        step = jnp.int32(-1)
        for spot, entry in enumerate(ORDER):
            if entry >= 0:
                step = jnp.where(position == spot, entry, step)
        return step

    def tick(position, carry):
        step = work_at(position)
        slot, w, group, away = split(jnp.maximum(step, 0))
        spot = position % 16

        @pl.when(step == 1)
        def _():
            act_wait(3, 0)
            on_up().start()
            to_mate(3, 0).start()
            act_wait(2, 0)
            to_mate(2, 0).start()

        @pl.when(step == 2)
        def _():
            act_wait(2, 1)
            on_down().start()
            to_mate(2, 1).start()
            act_wait(3, 1)
            to_mate(3, 1).start()

        @pl.when(step == 4)
        def _():
            for part in range(2):
                act_wait(6, part)
                to_mate(6, part).start()

        @pl.when((step == 1) | (step == 4) | (step == 5) | (step == 7))
        def _():
            act_wait(slot, 0)
            act_wait(slot, 1)

        @pl.when((step >= 0) & (step < 8))
        def _():
            for part in range(2):
                share_copy(slot, part).wait_recv()

        @pl.when(step == 0)
        def _():
            w_own.wait()
            w_others[0].wait_recv()

        @pl.when(step == 8)
        def _():
            w_others[1].wait_recv()
            w_others[2].wait_recv()

        @pl.when(step >= 0)
        def _():
            def one_tile(tile, c):
                column = pl.ds(pl.multiple_of(tile * 256, 256), 256)
                held[spot, :, column] = jnp.dot(
                    acts[slot], weights[w, :, column], preferred_element_type=F32
                )
                return c

            lax.fori_loop(0, tiles, one_tile, 0)

            @pl.when(away == 1)
            def _():
                chain_out[step, 0:rows] = held[spot, 0:rows].astype(BF16)
                chain_copy(step, 0).start()

            @pl.when(away == 3)
            def _():
                chain_out[step, rows:] = held[spot, rows:].astype(BF16)
                chain_copy(step, 1).start()

        two = work_at(position - HOP2)
        away_two = split(jnp.maximum(two, 0))[3]

        @pl.when((two >= 0) & (away_two == 2))
        def _():
            for part in range(2):
                pass_on(two, (position + 16 - HOP2) % 16, part)

        three = work_at(position - HOP3)
        away_three = split(jnp.maximum(three, 0))[3]

        @pl.when((three >= 0) & (away_three == 3))
        def _():
            pass_on(three, (position + 16 - HOP3) % 16, 0)

        @pl.when((three >= 0) & (away_three == 1))
        def _():
            pass_on(three, (position + 16 - HOP3) % 16, 1)

        four = work_at(position - HOP4)
        _, w_four, group_four, away_four = split(jnp.maximum(four, 0))

        @pl.when((four >= 0) & (away_four == 0))
        def _():
            which = group_four * 2 + w_four
            for part in range(2):
                chain_copy(four, part).wait_recv()
            last_out[which] = (
                held[(position + 16 - HOP4) % 16] + chain_in[four].astype(F32)
            ).astype(BF16)
            here, copy = last_copy(w_four, group_four)

            @pl.when(here)
            def _():
                last_in[zl, :, last_columns] = last_out[which]

            @pl.when(jnp.logical_not(here))
            def _():
                copy.start()

        return carry

    lax.fori_loop(0, len(ORDER) + HOP4, tick, 0)

    for zs in range(2):
        for cs in range(2):
            @pl.when((near == 0) | (zs != zl) | (cs != core))
            def _():
                remote(
                    last_out.at[0], last_in.at[zs, :, cs * half:(cs + 1) * half], last_send.at[0],
                    last_recv.at[zs * 2 + cs], sibling,
                ).wait_recv()

    for copy in w_others:
        copy.wait_send()
    for copy in kz_sends:
        copy.wait_send()
    for dz in range(4):
        for copy in kv_row(dz)[:2] + (kv_far(dz),):
            copy.wait_send()
        for dy in range(4):
            ks_copy(dz, dy).wait_send()
    for part in range(2):
        to_up(part).wait_send()
        to_down(part).wait_send()
        for slot in y_slot:
            to_mate(slot, part).wait_send()
        for slot in range(8):
            share_copy(slot, part).wait_send()
    on_up().wait_send()
    on_down().wait_send()

    def drain(step, carry):
        _, w, group, away = split(step)

        @pl.when(away != 0)
        def _():
            for part in range(2):
                chain_copy(step, part).wait_send()

        @pl.when(away == 0)
        def _():
            here, copy = last_copy(w, group)

            @pl.when(jnp.logical_not(here))
            def _():
                copy.wait_send()

        return carry

    lax.fori_loop(0, 16, drain, 0)


def per_device(
    queries, key_states, value_states, vertical_blocks, slash_offsets, positions, out_weight
):
    tokens, depth = queries.shape
    width = out_weight.shape[1]
    half = width // 2
    inverse_freq = 500000.0 ** (-np.arange(HD // 2) * (2.0 / HD))
    freq = jnp.asarray(np.tile(inverse_freq, (8, 2)), F32)
    anywhere = pl.BlockSpec(memory_space=pl.ANY)
    dma = pltpu.SemaphoreType.DMA
    pieces = pl.pallas_call(
        kernel,
        out_shape=jax.ShapeDtypeStruct((2, tokens, width), BF16),
        in_specs=[anywhere] * 3 + [pl.BlockSpec(memory_space=pltpu.VMEM)] + [anywhere] * 4,
        out_specs=pl.BlockSpec(memory_space=pltpu.VMEM),
        scratch_shapes=[
            pltpu.SMEM(vertical_blocks.shape[::-1], jnp.int32),
            pltpu.SMEM(slash_offsets.shape[::-1], jnp.int32),
            pltpu.SMEM(positions.shape, jnp.int32),
            pltpu.VMEM((tokens, depth), BF16),
            pltpu.VMEM((BLK, HD), BF16),
            pltpu.VMEM((BLK, HD), BF16),
            pltpu.VMEM((2, depth // HD, HD, BLK), BF16),
            pltpu.VMEM((32, 2, BLK, HD), BF16),
            pltpu.VMEM((8, tokens, 2 * depth), BF16),
            pltpu.VMEM((2, 2 * depth, half), BF16),
            pltpu.VMEM((16, tokens, half), F32),
            pltpu.VMEM((16, tokens, half), BF16),
            pltpu.VMEM((16, tokens, half), BF16),
            pltpu.VMEM((4, tokens, half), BF16),
            dma((6,)), dma, dma((3,)), dma((3,)),
            dma((4,)), dma((4,)), dma((4, 3)), dma((4, 4)), dma((4, 4)), dma((4, 4)),
            dma((8, 2)), dma((8, 2)), dma((8, 2)), dma((3, 2)), dma((8, 2)),
            dma((16, 2)), dma((16, 2)), dma((4,)), dma((4,)),
        ],
        compiler_params=pltpu.CompilerParams(
            collective_id=0, has_side_effects=True, vmem_limit_bytes=56 * 1024 * 1024
        ),
    )(
        vertical_blocks.T, slash_offsets.T, positions, freq, queries, key_states, value_states,
        out_weight,
    ).astype(F32)
    return (pieces[0] + pieces[1]).astype(BF16)


def solution(mesh):
    placed = (
        P("ctx", "head"),
        P("ctx", None),
        P("ctx", None),
        P("head", None),
        P("head", None),
        P("ctx"),
        P("head", "ctx"),
    )
    return jax.shard_map(
        per_device, mesh=mesh, in_specs=placed, out_specs=P("head", "ctx"), check_vma=False
    )
```

```python
import math

import jax
import jax.numpy as jnp
import numpy as np
from jax import lax
from jax.experimental import pallas as pl
from jax.experimental.pallas import tpu as pltpu
from jax.sharding import PartitionSpec as P

HD = 128
BLK = 128
MESH = pl.DeviceIdType.MESH
BF16 = jnp.bfloat16
F32 = jnp.float32

HOP2, HOP3, HOP4 = 4, 9, 14
PRODUCTS = 32
PAUSES = 6
CHUNKS = 4


def place():
    ctx = lax.axis_index("ctx")
    head = lax.axis_index("head")
    return ctx // 4, ctx % 4, head // 4, (head // 2) % 2, head % 2


def device(zh, y, x, zl, core):
    return {"ctx": (zh % 4) * 4 + y % 4, "head": (x % 4) * 4 + zl * 2 + core}


def remote(src, dst, send, recv, where):
    return pltpu.make_async_remote_copy(
        src_ref=src, dst_ref=dst, send_sem=send, recv_sem=recv, device_id=where, device_id_type=MESH
    )


def turned(states, cosine, sine):
    states = states.astype(F32)
    return states * cosine + pltpu.roll(states, HD // 2, 1) * sine


def kernel(
    vert_in, slash_in, pos_in, freq_ref, q_in, k_ref, v_ref, w_ref, low_in, high_in,
    vert_ref, slash_ref, pos_ref, q_ref, k_own, v_own, q_rot, kv, acts, weights, held, chain_out,
    chain_in, last_out,
    own_sem, w_sem, w_send, w_recv, kz_send, kz_recv, ky_send, ky_recv, ks_send, ks_recv,
    act_recv, as_send, as_recv, z_send, y_send, chain_send, chain_recv, last_send, last_recv,
):
    zh, y, x, zl, core = place()
    mate = 3 - y
    pair = y + 1 - 2 * (y % 2)
    z_up = device(zh + 1, y, x, zl, core)
    z_down = device(zh + 3, y, x, zl, core)
    y_up = device(zh, y + 1, x, zl, core)
    y_down = device(zh, y + 3, x, zl, core)
    y_mate = device(zh, mate, x, zl, core)
    y_pair = device(zh, pair, x, zl, core)
    y_pair_sibling = device(zh, pair, x, zl, 1 - core)
    x_up = device(zh, y, x + 1, zl, core)
    x_down = device(zh, y, x + 3, zl, core)
    sibling = device(zh, y, x, zl, 1 - core)
    half = weights.shape[2]
    depth = q_ref.shape[1]
    rows = acts.shape[1] // 2
    chunk = acts.shape[1] // CHUNKS
    heads = q_ref.shape[1] // HD

    kv_column = pl.multiple_of((x * 2 + zl) * HD, HD)
    own_rows = pl.ds(pl.multiple_of(core * BLK, BLK), BLK)
    small = [
        pltpu.make_async_copy(src, dst, own_sem.at[i])
        for i, (src, dst) in enumerate((
            (pos_in, pos_ref),
            (k_ref.at[own_rows, pl.ds(kv_column, HD)], k_own),
            (v_ref.at[own_rows, pl.ds(kv_column, HD)], v_own),
            (q_in, q_ref),
            (vert_in, vert_ref),
            (slash_in, slash_ref),
        ))
    ]
    for copy in small:
        copy.start()

    depth_here = pl.ds(pl.multiple_of(core * depth, depth), depth)

    def w_part(which, start=0, size=half):
        return w_ref.at[:, pl.ds(pl.multiple_of(which * half + start, 256), size)]

    w_own = pltpu.make_async_copy(w_part(core), weights.at[0, depth_here], w_sem)
    w_others = [remote(w_part(1 - core), weights.at[0, depth_here], w_send.at[0], w_recv.at[0], sibling)]
    for start in (0, 256):
        for which, where in ((core, y_pair), (1 - core, y_pair_sibling)):
            i = len(w_others)
            w_others.append(remote(
                w_part(which, start, 256), weights.at[1, depth_here, pl.ds(start, 256)],
                w_send.at[i], w_recv.at[i], where,
            ))
    w_own.start()

    token_row = zl * 2 + core
    near = jnp.where((token_row == y) | (token_row == mate), 1, 0)
    source_row = jnp.where(near == 1, y, pair)

    barrier = pltpu.get_barrier_semaphore()

    def greet(where):
        pl.semaphore_signal(barrier, inc=1, device_id=where, device_id_type=MESH)

    for where in (z_up, z_down, y_up, y_down, x_up, x_down, sibling, y_pair_sibling):
        greet(where)
    for zs in range(2):
        for cs in range(2):
            @pl.when((near == 0) | (zs != zl) | (cs != core))
            def _():
                greet(device(zh, source_row, x, zs, cs))

    def block(dz, dy, which=core):
        return (((zh + dz) % 4) * 4 + (y + dy) % 4) * 2 + which

    mine = block(0, 0)
    small[0].wait()
    lane = lax.broadcasted_iota(jnp.int32, (BLK, HD), 1)
    row = lax.broadcasted_iota(jnp.int32, (BLK, HD), 0)
    first = lane < HD // 2
    start = jnp.where(first, pos_ref[0], pos_ref[BLK])
    angles = (start + row).astype(F32) * freq_ref[0:1, :]
    cosine = jnp.cos(angles)
    sine = jnp.sin(angles)
    cosine_other = pltpu.roll(cosine, HD // 2, 1)
    sine_other = pltpu.roll(sine, HD // 2, 1)
    tables = (
        (jnp.where(first, cosine, cosine_other), jnp.where(first, -sine, sine_other)),
        (jnp.where(first, cosine_other, cosine), jnp.where(first, -sine_other, sine)),
    )
    small[1].wait()
    small[2].wait()
    kv[mine, 0] = turned(
        k_own[...], *(jnp.where(core == 0, one, two) for one, two in zip(*tables))
    ).astype(BF16)
    kv[mine, 1] = v_own[...].astype(F32).T.astype(BF16)
    pl.semaphore_wait(barrier, 12 - near)

    def kz_copy(dz_there, index, where):
        return remote(kv.at[mine], kv.at[mine], kz_send.at[index], kz_recv.at[dz_there], where)

    def kz_on(dz, part, where):
        here = kv.at[block(dz, 0), part]
        return remote(here, here, kz_send.at[2 + part], kz_recv.at[2 + part], where)

    def ky_copy(dz, dy, index, there, where):
        here = kv.at[block(dz, dy)]
        return remote(here, here, ky_send.at[dz, index], ky_recv.at[dz, there], where)

    def ks_copy(dz, dy):
        here = kv.at[block(dz, dy)]
        return remote(here, here, ks_send.at[dz, dy], ks_recv.at[dz, dy], sibling)

    def kv_row(dz):
        return (ky_copy(dz, 0, 0, 3, y_up), ky_copy(dz, 0, 1, 1, y_down), ks_copy(dz, 0))

    def kv_far(dz):
        if dz < 2:
            return ky_copy(dz, 3, 2, 2, y_up)
        return ky_copy(dz, 1, 2, 2, y_down)

    kz_sends = (kz_copy(1, 0, z_up), kz_copy(0, 1, z_down), kz_on(3, 0, z_up), kz_on(1, 1, z_down))
    kz_sends[0].start()
    kz_sends[1].start()
    for copy in kv_row(0):
        copy.start()

    scale = math.log2(math.e) / math.sqrt(HD)
    small[3].wait()
    for part in range(2):
        cosine, sine = (table * scale for table in tables[part])
        for h in range(heads):
            states = q_ref[part * BLK:(part + 1) * BLK, h * HD:(h + 1) * HD]
            q_rot[part, h] = turned(states, cosine, sine).T.astype(BF16)
    small[4].wait()
    small[5].wait()

    kz_sends[1].wait_recv()
    kz_sends[3].start()
    for copy in kv_row(1):
        copy.start()
    kz_sends[0].wait_recv()
    kz_sends[2].start()
    for copy in kv_row(3):
        copy.start()

    def kv_near(dz):
        for dy in (3, 1):
            ky_copy(dz, dy, 0, dy, sibling).wait_recv()
            if (dy == 3) == (dz < 2):
                kv_far(dz).start()
            ks_copy(dz, dy).start()

    kv_near(0)
    kz_sends[2].wait_recv()
    kz_sends[3].wait_recv()
    for copy in kv_row(2):
        copy.start()
    kv_near(1)
    kv_near(3)
    kv_near(2)
    for copy in w_others:
        copy.start()
    for dz in range(4):
        ky_copy(dz, 2, 0, 2, sibling).wait_recv()
        ks_copy(dz, 2).start()
    for dz in range(4):
        for dy in range(4):
            ks_copy(dz, dy).wait_recv()

    def act_at(slot, part):
        return acts.at[slot, pl.ds(part * chunk, chunk), depth_here]

    def act_copy(src_slot, dst_slot, part, send, where):
        return remote(
            act_at(src_slot, part), act_at(dst_slot, part), send, act_recv.at[dst_slot, part], where
        )

    def share_copy(slot, part):
        here = act_at(slot, part)
        return remote(here, here, as_send.at[slot, part], as_recv.at[slot, part], sibling)

    def act_wait(slot, part):
        act_copy(slot, slot, part, z_send.at[0, 0], sibling).wait_recv()
        share_copy(slot, part).start()

    to_up = lambda part: act_copy(0, 3, part, z_send.at[0, part], z_up)
    to_down = lambda part: act_copy(0, 2, part, z_send.at[1, part], z_down)
    on_up = lambda part: act_copy(3, 6, part, z_send.at[2, part], z_up)
    on_down = lambda part: act_copy(2, 6, part, z_send.at[2, part], z_down)
    y_slot = {0: 1, 2: 4, 3: 5, 6: 7}
    to_mate = lambda slot, part: act_copy(slot, y_slot[slot], part, y_send.at[slot, part], y_mate)

    ctx = zh * 4 + y

    def attend(part):
        here = ctx * 2 + part

        def one_head(h, carry):
            column = pl.ds(pl.multiple_of(core * depth + h * HD, HD), HD)
            vertical = [vert_ref[s, h] for s in range(4)]
            blocks = [here] + vertical
            bias = [None] + [jnp.where(b < here, 0.0, -1e30) for b in vertical]
            for s in range(1, 4):
                b = here - slash_ref[s, h]
                seen = (b == vertical[0]) | (b == vertical[1]) | (b == vertical[2]) | (b == vertical[3])
                blocks.append(jnp.maximum(b, 0))
                bias.append(jnp.where((b >= 0) & jnp.logical_not(seen), 0.0, -1e30))
            keys = jnp.concatenate([kv[b, 0] for b in blocks], axis=0)
            values = jnp.concatenate([kv[b, 1] for b in blocks], axis=1)
            scores = jnp.dot(keys, q_rot[part, h], preferred_element_type=F32)
            tiles_of = [scores[s * BLK:(s + 1) * BLK] for s in range(8)]
            key_row = lax.broadcasted_iota(jnp.int32, (BLK, BLK), 0)
            query_row = lax.broadcasted_iota(jnp.int32, (BLK, BLK), 1)
            tiles_of[0] = jnp.where(key_row <= query_row, tiles_of[0], -1e30)
            top = jnp.max(tiles_of[0], axis=0, keepdims=True)
            for s in range(1, 8):
                top = jnp.maximum(top, jnp.max(tiles_of[s], axis=0, keepdims=True) + bias[s])
            powers = [jnp.exp2(tiles_of[0] - top)]
            for s in range(1, 8):
                powers.append(jnp.exp2(tiles_of[s] - (top - bias[s])))
            total = sum(jnp.sum(p, axis=0, keepdims=True) for p in powers)
            mixed = jnp.dot(
                values, jnp.concatenate([p.astype(BF16) for p in powers], axis=0),
                preferred_element_type=F32,
            )
            acts[0, part * BLK:(part + 1) * BLK, column] = (mixed * (1.0 / total)).T.astype(BF16)
            return carry

        lax.fori_loop(0, heads, one_head, 0, unroll=4)

    for part in range(2):
        attend(part)
        to_up(part).start()
        to_down(part).start()
        for q in (2 * part, 2 * part + 1):
            to_mate(0, q).start()
            share_copy(0, q).start()

    def send_later(q):
        to_up(q - 2).wait_send()
        to_down(q - 2).wait_send()
        to_up(q).start()
        to_down(q).start()

    def forward(q):
        act_wait(3, q)
        to_mate(3, q).start()
        act_wait(2, q)
        to_mate(2, q).start()

    def forward_far(q):
        act_wait(6, q)
        to_mate(6, q).start()

    def split(step):
        third = lax.shift_right_arithmetic((step - 6) * 11, 5)
        slot = jnp.where(step < 4, lax.shift_right_arithmetic(step, 1), step - 4)
        tile = jnp.where(step < 4, lax.bitwise_and(step, 1), 2)
        slot = jnp.where(step >= 6, 2 + third, slot)
        tile = jnp.where(step >= 6, step - 6 - 3 * third, tile)
        slot = jnp.where(step >= 21, step - 21, slot)
        tile = jnp.where(step >= 21, 3, tile)
        slot = jnp.where(step >= 28, 7, slot)
        tile = jnp.where(step >= 28, step - 28, tile)
        ahead = jnp.where(slot < 2, 0, jnp.where(slot < 6, 1 + 2 * lax.bitwise_and(slot, 1), 2))
        group = jnp.where(
            slot < 2, slot, jnp.where(slot < 6, lax.shift_right_arithmetic(slot - 2, 1), slot - 6)
        )
        return slot, tile, group, lax.bitwise_and(x + 8 - zh - ahead, 3)

    def chain_copy(step, part):
        here = pl.ds(part * rows, rows)
        return remote(
            chain_out.at[step, here], chain_in.at[step, here], chain_send.at[step, part],
            chain_recv.at[step, part], x_down if part else x_up,
        )

    def last_place(tile, group):
        row = jnp.where(group == 0, y, mate)
        column = jnp.where(tile < 2, y, pair)
        here = (tile < 2) & (row // 2 == zl) & (row % 2 == core)
        columns = pl.ds(pl.multiple_of(core * half + (tile % 2) * 256, 256), 256)
        return here, device(zh, column, x, row // 2, row % 2), group * 4 + tile, columns

    def last_copy(tile, group, zs):
        _, where, which, columns = last_place(tile, group)
        return remote(
            last_out.at[which], (low_in, high_in)[zs].at[:, columns], last_send.at[which],
            last_recv.at[zs * 2 + core, tile % 2], where,
        )

    def send_last(tile, group):
        here, _, which, columns = last_place(tile, group)
        for zs, target in enumerate((low_in, high_in)):
            @pl.when(here & (zl == zs))
            def _():
                target[:, columns] = last_out[which]

            @pl.when(jnp.logical_not(here) & (zl == zs))
            def _():
                last_copy(tile, group, zs).start()

    def pass_on(step, spot, part):
        here = slice(part * rows, (part + 1) * rows)
        chain_copy(step, part).wait_recv()
        chain_out[step, here] = (held[spot, here] + chain_in[step, here].astype(F32)).astype(BF16)
        chain_copy(step, part).start()

    def work_at(position):
        step = jnp.where(position < 2, position, -1)
        step = jnp.where((position >= 5) & (position < 7), position - 3, step)
        step = jnp.where((position >= 10) & (position < PRODUCTS + PAUSES), position - PAUSES, step)
        return step

    def tick(position, carry):
        step = work_at(position)
        slot, tile, group, away = split(jnp.maximum(step, 0))
        spot = lax.bitwise_and(position, 15)

        @pl.when(step == 2)
        def _():
            forward(1)

        @pl.when(step == 4)
        def _():
            forward(2)
            on_up(0).start()
            on_down(2).start()

        @pl.when(step == 6)
        def _():
            forward(3)
            on_up(1).start()
            on_down(3).start()

        @pl.when(step == 10)
        def _():
            forward_far(0)
            forward_far(2)

        @pl.when(step == 12)
        def _():
            forward_far(1)
            forward_far(3)

        @pl.when((step == 2) | (step == 12) | (step == 15) | (step == 28))
        def _():
            for q in range(CHUNKS):
                act_wait(slot, q)

        @pl.when((step >= 0) & (tile == 0))
        def _():
            for q in range(CHUNKS):
                share_copy(slot, q).wait_recv()

        @pl.when(step == 0)
        def _():
            w_own.wait()
            w_others[0].wait_recv()

        @pl.when(step == 4)
        def _():
            w_others[1].wait_recv()
            w_others[2].wait_recv()

        @pl.when(step == 21)
        def _():
            w_others[3].wait_recv()
            w_others[4].wait_recv()

        @pl.when(step >= 0)
        def _():
            column = pl.ds(pl.multiple_of(lax.bitwise_and(tile, 1) * 256, 256), 256)
            held[spot] = jnp.dot(
                acts[slot], weights[lax.shift_right_arithmetic(tile, 1), :, column], preferred_element_type=F32
            )

            @pl.when(away == 1)
            def _():
                chain_out[step, 0:rows] = held[spot, 0:rows].astype(BF16)
                chain_copy(step, 0).start()

            @pl.when(away == 3)
            def _():
                chain_out[step, rows:] = held[spot, rows:].astype(BF16)
                chain_copy(step, 1).start()

        @pl.when(step == 0)
        def _():
            send_later(2)

        @pl.when(step == 1)
        def _():
            forward(0)
            send_later(3)

        two = work_at(position - HOP2)
        away_two = split(jnp.maximum(two, 0))[3]

        @pl.when((two >= 0) & (away_two == 2))
        def _():
            for part in range(2):
                pass_on(two, lax.bitwise_and(position + 16 - HOP2, 15), part)

        three = work_at(position - HOP3)
        away_three = split(jnp.maximum(three, 0))[3]

        @pl.when((three >= 0) & (away_three == 3))
        def _():
            pass_on(three, lax.bitwise_and(position + 16 - HOP3, 15), 0)

        @pl.when((three >= 0) & (away_three == 1))
        def _():
            pass_on(three, lax.bitwise_and(position + 16 - HOP3, 15), 1)

        four = work_at(position - HOP4)
        _, tile_four, group_four, away_four = split(jnp.maximum(four, 0))

        @pl.when((four >= 0) & (away_four == 0))
        def _():
            which = group_four * 4 + tile_four
            for part in range(2):
                chain_copy(four, part).wait_recv()
            last_out[which] = (
                held[lax.bitwise_and(position + 16 - HOP4, 15)] + chain_in[four].astype(F32)
            ).astype(BF16)
            send_last(tile_four, group_four)

        return carry

    lax.fori_loop(0, PRODUCTS + PAUSES + HOP4, tick, 0)

    for copy in w_others:
        copy.wait_send()
    for copy in kz_sends:
        copy.wait_send()
    for dz in range(4):
        for copy in kv_row(dz)[:2] + (kv_far(dz),):
            copy.wait_send()
        for dy in range(4):
            ks_copy(dz, dy).wait_send()
    for q in range(CHUNKS):
        if q >= 2:
            to_up(q).wait_send()
            to_down(q).wait_send()
        for slot in y_slot:
            to_mate(slot, q).wait_send()
        for slot in range(8):
            share_copy(slot, q).wait_send()
        (on_up if q < CHUNKS // 2 else on_down)(q).wait_send()

    def drain(step, carry):
        _, tile, group, away = split(step)

        @pl.when(away != 0)
        def _():
            for part in range(2):
                chain_copy(step, part).wait_send()

        @pl.when((away == 0) & jnp.logical_not(last_place(tile, group)[0]))
        def _():
            last_copy(tile, group, 0).wait_send()

        return carry

    lax.fori_loop(0, PRODUCTS, drain, 0)

    for zs in range(2):
        for cs in range(2):
            @pl.when((near == 0) | (zs != zl) | (cs != core))
            def _():
                for part in range(2):
                    column = cs * half + part * 256
                    remote(
                        last_out.at[0], (low_in, high_in)[zs].at[:, column:column + 256],
                        last_send.at[0], last_recv.at[zs * 2 + cs, part], sibling,
                    ).wait_recv()


def per_device(
    queries, key_states, value_states, vertical_blocks, slash_offsets, positions, out_weight
):
    tokens, depth = queries.shape
    width = out_weight.shape[1]
    half = width // 2
    inverse_freq = 500000.0 ** (-np.arange(HD // 2) * (2.0 / HD))
    freq = jnp.asarray(np.tile(inverse_freq, (8, 2)), F32)
    anywhere = pl.BlockSpec(memory_space=pl.ANY)
    dma = pltpu.SemaphoreType.DMA
    low, high = pl.pallas_call(
        kernel,
        out_shape=[jax.ShapeDtypeStruct((tokens, width), BF16)] * 2,
        in_specs=[anywhere] * 3 + [pl.BlockSpec(memory_space=pltpu.VMEM)] + [anywhere] * 4,
        out_specs=[pl.BlockSpec(memory_space=pltpu.VMEM)] * 2,
        scratch_shapes=[
            pltpu.SMEM(vertical_blocks.shape[::-1], jnp.int32),
            pltpu.SMEM(slash_offsets.shape[::-1], jnp.int32),
            pltpu.SMEM(positions.shape, jnp.int32),
            pltpu.VMEM((tokens, depth), BF16),
            pltpu.VMEM((BLK, HD), BF16),
            pltpu.VMEM((BLK, HD), BF16),
            pltpu.VMEM((2, depth // HD, HD, BLK), BF16),
            pltpu.VMEM((32, 2, BLK, HD), BF16),
            pltpu.VMEM((8, tokens, 2 * depth), BF16),
            pltpu.VMEM((2, 2 * depth, half), BF16),
            pltpu.VMEM((16, tokens, 256), F32),
            pltpu.VMEM((PRODUCTS, tokens, 256), BF16),
            pltpu.VMEM((PRODUCTS, tokens, 256), BF16),
            pltpu.VMEM((8, tokens, 256), BF16),
            dma((6,)), dma, dma((5,)), dma((5,)),
            dma((4,)), dma((4,)), dma((4, 3)), dma((4, 4)), dma((4, 4)), dma((4, 4)),
            dma((8, CHUNKS)), dma((8, CHUNKS)), dma((8, CHUNKS)), dma((3, CHUNKS)), dma((8, CHUNKS)),
            dma((PRODUCTS, 2)), dma((PRODUCTS, 2)), dma((8,)), dma((4, 2)),
        ],
        compiler_params=pltpu.CompilerParams(
            collective_id=0, has_side_effects=True, vmem_limit_bytes=56 * 1024 * 1024
        ),
    )(
        vertical_blocks.T, slash_offsets.T, positions, freq, queries, key_states, value_states,
        out_weight,
    )
    return (low.astype(F32) + high.astype(F32)).astype(BF16)


def solution(mesh):
    placed = (
        P("ctx", "head"),
        P("ctx", None),
        P("ctx", None),
        P("head", None),
        P("head", None),
        P("ctx"),
        P("head", "ctx"),
    )
    return jax.shard_map(
        per_device, mesh=mesh, in_specs=placed, out_specs=P("head", "ctx"), check_vma=False
    )
```

```python
import math

import jax
import jax.numpy as jnp
import numpy as np
from jax import lax
from jax.experimental import pallas as pl
from jax.experimental.pallas import tpu as pltpu
from jax.sharding import PartitionSpec as P

HD = 128
BLK = 128
MESH = pl.DeviceIdType.MESH
BF16 = jnp.bfloat16
F32 = jnp.float32

HOP2, HOP3, HOP4 = 4, 9, 14
PRODUCTS = 32
FLUSH = 2
PAUSES = 6 + FLUSH
CHUNKS = 4


def place():
    ctx = lax.axis_index("ctx")
    head = lax.axis_index("head")
    return ctx // 4, ctx % 4, head // 4, (head // 2) % 2, head % 2


def device(zh, y, x, zl, core):
    return {"ctx": (zh % 4) * 4 + y % 4, "head": (x % 4) * 4 + zl * 2 + core}


def remote(src, dst, send, recv, where):
    return pltpu.make_async_remote_copy(
        src_ref=src, dst_ref=dst, send_sem=send, recv_sem=recv, device_id=where, device_id_type=MESH
    )


def turned(states, cosine, sine):
    states = states.astype(F32)
    return states * cosine + pltpu.roll(states, HD // 2, 1) * sine


def kernel(
    vert_in, slash_in, pos_in, freq_ref, q_in, k_ref, v_ref, w_ref, low_in, high_in,
    vert_ref, slash_ref, pos_ref, q_ref, k_own, v_own, q_rot, kv, acts, weights, held, chain_out,
    chain_in, last_out,
    own_sem, w_sem, w_send, w_recv, kz_send, kz_recv, ky_send, ky_recv, ks_send, ks_recv,
    act_recv, as_send, as_recv, z_send, y_send, chain_send, chain_recv, last_send, last_recv,
):
    zh, y, x, zl, core = place()
    mate = 3 - y
    pair = y + 1 - 2 * (y % 2)
    z_up = device(zh + 1, y, x, zl, core)
    z_down = device(zh + 3, y, x, zl, core)
    y_up = device(zh, y + 1, x, zl, core)
    y_down = device(zh, y + 3, x, zl, core)
    y_mate = device(zh, mate, x, zl, core)
    y_pair = device(zh, pair, x, zl, core)
    y_pair_sibling = device(zh, pair, x, zl, 1 - core)
    x_up = device(zh, y, x + 1, zl, core)
    x_down = device(zh, y, x + 3, zl, core)
    sibling = device(zh, y, x, zl, 1 - core)
    half = weights.shape[2]
    depth = q_ref.shape[1]
    rows = acts.shape[1] // 2
    chunk = acts.shape[1] // CHUNKS
    heads = q_ref.shape[1] // HD

    kv_column = pl.multiple_of((x * 2 + zl) * HD, HD)
    own_rows = pl.ds(pl.multiple_of(core * BLK, BLK), BLK)
    small = [
        pltpu.make_async_copy(src, dst, own_sem.at[i])
        for i, (src, dst) in enumerate((
            (pos_in, pos_ref),
            (k_ref.at[own_rows, pl.ds(kv_column, HD)], k_own),
            (v_ref.at[own_rows, pl.ds(kv_column, HD)], v_own),
            (q_in, q_ref),
            (vert_in, vert_ref),
            (slash_in, slash_ref),
        ))
    ]
    for copy in small:
        copy.start()

    depth_here = pl.ds(pl.multiple_of(core * depth, depth), depth)

    def w_part(which, start=0, size=half):
        return w_ref.at[:, pl.ds(pl.multiple_of(which * half + start, 256), size)]

    w_own = pltpu.make_async_copy(w_part(core), weights.at[0, depth_here], w_sem)
    w_others = [remote(w_part(1 - core), weights.at[0, depth_here], w_send.at[0], w_recv.at[0], sibling)]
    for start in (0, 256):
        for which, where in ((core, y_pair), (1 - core, y_pair_sibling)):
            i = len(w_others)
            w_others.append(remote(
                w_part(which, start, 256), weights.at[1, depth_here, pl.ds(start, 256)],
                w_send.at[i], w_recv.at[i], where,
            ))
    w_own.start()

    token_row = zl * 2 + core
    near = jnp.where((token_row == y) | (token_row == mate), 1, 0)
    source_row = jnp.where(near == 1, y, pair)

    barrier = pltpu.get_barrier_semaphore()

    def greet(where):
        pl.semaphore_signal(barrier, inc=1, device_id=where, device_id_type=MESH)

    for where in (z_up, z_down, y_up, y_down, x_up, x_down, sibling, y_pair_sibling):
        greet(where)
    for zs in range(2):
        for cs in range(2):
            @pl.when((near == 0) | (zs != zl) | (cs != core))
            def _():
                greet(device(zh, source_row, x, zs, cs))

    def block(dz, dy, which=core):
        return (((zh + dz) % 4) * 4 + (y + dy) % 4) * 2 + which

    mine = block(0, 0)
    small[0].wait()
    lane = lax.broadcasted_iota(jnp.int32, (BLK, HD), 1)
    row = lax.broadcasted_iota(jnp.int32, (BLK, HD), 0)
    first = lane < HD // 2
    start = jnp.where(first, pos_ref[0], pos_ref[BLK])
    angles = (start + row).astype(F32) * freq_ref[0:1, :]
    cosine = jnp.cos(angles)
    sine = jnp.sin(angles)
    cosine_other = pltpu.roll(cosine, HD // 2, 1)
    sine_other = pltpu.roll(sine, HD // 2, 1)
    tables = (
        (jnp.where(first, cosine, cosine_other), jnp.where(first, -sine, sine_other)),
        (jnp.where(first, cosine_other, cosine), jnp.where(first, -sine_other, sine)),
    )
    small[1].wait()
    small[2].wait()
    kv[mine, 0] = turned(
        k_own[...], *(jnp.where(core == 0, one, two) for one, two in zip(*tables))
    ).astype(BF16)
    kv[mine, 1] = v_own[...].astype(F32).T.astype(BF16)
    pl.semaphore_wait(barrier, 12 - near)

    def all_of(ref, send, recv):
        return remote(ref, ref, send, recv, sibling)

    def kz_copy(dz_there, index, where):
        return remote(kv.at[mine], kv.at[mine], kz_send.at[index], kz_recv.at[dz_there], where)

    def kz_on(dz, part, where):
        here = kv.at[block(dz, 0), part]
        return remote(here, here, kz_send.at[2 + part], kz_recv.at[2 + part], where)

    def ky_copy(dz, dy, index, there, where):
        here = kv.at[block(dz, dy)]
        return remote(here, here, ky_send, ky_recv.at[dz, there], where)

    def ks_copy(dz, dy):
        here = kv.at[block(dz, dy)]
        return remote(here, here, ks_send, ks_recv, sibling)

    def kv_row(dz):
        return (ky_copy(dz, 0, 0, 3, y_up), ky_copy(dz, 0, 1, 1, y_down), ks_copy(dz, 0))

    def kv_far(dz):
        if dz < 2:
            return ky_copy(dz, 3, 2, 2, y_up)
        return ky_copy(dz, 1, 2, 2, y_down)

    kz_sends = (kz_copy(1, 0, z_up), kz_copy(0, 1, z_down), kz_on(3, 0, z_up), kz_on(1, 1, z_down))
    kz_sends[0].start()
    kz_sends[1].start()
    for copy in kv_row(0):
        copy.start()

    scale = math.log2(math.e) / math.sqrt(HD)
    small[3].wait()
    for part in range(2):
        cosine, sine = (table * scale for table in tables[part])
        for h in range(heads):
            states = q_ref[part * BLK:(part + 1) * BLK, h * HD:(h + 1) * HD]
            q_rot[part, h] = turned(states, cosine, sine).T.astype(BF16)
    small[4].wait()
    small[5].wait()

    kz_sends[1].wait_recv()
    kz_sends[3].start()
    for copy in kv_row(1):
        copy.start()
    kz_sends[0].wait_recv()
    kz_sends[2].start()
    for copy in kv_row(3):
        copy.start()

    def kv_near(dz):
        for dy in (3, 1):
            ky_copy(dz, dy, 0, dy, sibling).wait_recv()
            if (dy == 3) == (dz < 2):
                kv_far(dz).start()
            ks_copy(dz, dy).start()

    kv_near(0)
    kz_sends[2].wait_recv()
    kz_sends[3].wait_recv()
    for copy in kv_row(2):
        copy.start()
    kv_near(1)
    kv_near(3)
    kv_near(2)
    for copy in w_others:
        copy.start()
    for dz in range(4):
        ky_copy(dz, 2, 0, 2, sibling).wait_recv()
        ks_copy(dz, 2).start()
    all_of(kv.at[pl.ds(0, 16)], ks_send, ks_recv).wait_recv()

    def act_at(slot, part):
        return acts.at[slot, pl.ds(part * chunk, chunk), depth_here]

    def act_copy(src_slot, dst_slot, part, send, where):
        return remote(
            act_at(src_slot, part), act_at(dst_slot, part), send, act_recv.at[dst_slot, part], where
        )

    def share_copy(slot, part):
        here = act_at(slot, part)
        return remote(here, here, as_send, as_recv.at[slot, part], sibling)

    def act_wait(slot, part):
        act_copy(slot, slot, part, z_send.at[0, 0], sibling).wait_recv()
        share_copy(slot, part).start()

    to_up = lambda part: act_copy(0, 3, part, z_send.at[0, part], z_up)
    to_down = lambda part: act_copy(0, 2, part, z_send.at[1, part], z_down)
    on_up = lambda part: act_copy(3, 6, part, z_send.at[2, part], z_up)
    on_down = lambda part: act_copy(2, 6, part, z_send.at[2, part], z_down)
    y_slot = {0: 1, 2: 4, 3: 5, 6: 7}
    to_mate = lambda slot, part: act_copy(slot, y_slot[slot], part, y_send, y_mate)

    ctx = zh * 4 + y

    def attend(part):
        here = ctx * 2 + part

        def one_head(h, carry):
            column = pl.ds(pl.multiple_of(core * depth + h * HD, HD), HD)
            vertical = [vert_ref[s, h] for s in range(4)]
            blocks = [here] + vertical
            bias = [None] + [jnp.where(b < here, 0.0, -1e30) for b in vertical]
            for s in range(1, 4):
                b = here - slash_ref[s, h]
                seen = (b == vertical[0]) | (b == vertical[1]) | (b == vertical[2]) | (b == vertical[3])
                blocks.append(jnp.maximum(b, 0))
                bias.append(jnp.where((b >= 0) & jnp.logical_not(seen), 0.0, -1e30))
            keys = jnp.concatenate([kv[b, 0] for b in blocks], axis=0)
            values = jnp.concatenate([kv[b, 1] for b in blocks], axis=1)
            scores = jnp.dot(keys, q_rot[part, h], preferred_element_type=F32)
            tiles_of = [scores[s * BLK:(s + 1) * BLK] for s in range(8)]
            key_row = lax.broadcasted_iota(jnp.int32, (BLK, BLK), 0)
            query_row = lax.broadcasted_iota(jnp.int32, (BLK, BLK), 1)
            tiles_of[0] = jnp.where(key_row <= query_row, tiles_of[0], -1e30)
            top = jnp.max(tiles_of[0], axis=0, keepdims=True)
            for s in range(1, 8):
                top = jnp.maximum(top, jnp.max(tiles_of[s], axis=0, keepdims=True) + bias[s])
            powers = [jnp.exp2(tiles_of[0] - top)]
            for s in range(1, 8):
                powers.append(jnp.exp2(tiles_of[s] - (top - bias[s])))
            total = sum(jnp.sum(p, axis=0, keepdims=True) for p in powers)
            mixed = jnp.dot(
                values, jnp.concatenate([p.astype(BF16) for p in powers], axis=0),
                preferred_element_type=F32,
            )
            acts[0, part * BLK:(part + 1) * BLK, column] = (mixed * (1.0 / total)).T.astype(BF16)
            return carry

        lax.fori_loop(0, heads, one_head, 0, unroll=8)

    for part in range(2):
        attend(part)
        to_up(part).start()
        to_down(part).start()
        for q in (2 * part, 2 * part + 1):
            to_mate(0, q).start()
            share_copy(0, q).start()

    def send_later(q):
        to_up(q - 2).wait_send()
        to_down(q - 2).wait_send()
        to_up(q).start()
        to_down(q).start()

    def forward(q):
        act_wait(3, q)
        to_mate(3, q).start()
        act_wait(2, q)
        to_mate(2, q).start()

    def forward_far(q):
        act_wait(6, q)
        to_mate(6, q).start()

    def split(step):
        third = lax.shift_right_arithmetic((step - 6) * 11, 5)
        slot = jnp.where(step < 4, lax.shift_right_arithmetic(step, 1), step - 4)
        tile = jnp.where(step < 4, lax.bitwise_and(step, 1), 2)
        slot = jnp.where(step >= 6, 2 + third, slot)
        tile = jnp.where(step >= 6, step - 6 - 3 * third, tile)
        slot = jnp.where(step >= 21, step - 21, slot)
        tile = jnp.where(step >= 21, 3, tile)
        slot = jnp.where(step >= 28, 7, slot)
        tile = jnp.where(step >= 28, step - 28, tile)
        ahead = jnp.where(slot < 2, 0, jnp.where(slot < 6, 1 + 2 * lax.bitwise_and(slot, 1), 2))
        group = jnp.where(
            slot < 2, slot, jnp.where(slot < 6, lax.shift_right_arithmetic(slot - 2, 1), slot - 6)
        )
        return slot, tile, group, lax.bitwise_and(x + 8 - zh - ahead, 3)

    def chain_copy(step, part):
        here = pl.ds(part * rows, rows)
        return remote(
            chain_out.at[step, here], chain_in.at[step, here], chain_send,
            chain_recv.at[step, part], x_down if part else x_up,
        )

    def last_place(tile, group):
        row = jnp.where(group == 0, y, mate)
        column = jnp.where(tile < 2, y, pair)
        here = (tile < 2) & (row // 2 == zl) & (row % 2 == core)
        columns = pl.ds(pl.multiple_of(core * half + (tile % 2) * 256, 256), 256)
        return here, device(zh, column, x, row // 2, row % 2), group * 4 + tile, columns

    def last_copy(tile, group, zs):
        _, where, which, columns = last_place(tile, group)
        return remote(
            last_out.at[which], (low_in, high_in)[zs].at[:, columns], last_send,
            last_recv.at[zs * 2 + core, tile % 2], where,
        )

    def send_last(tile, group):
        here, _, which, columns = last_place(tile, group)
        for zs, target in enumerate((low_in, high_in)):
            @pl.when(here & (zl == zs))
            def _():
                target[:, columns] = last_out[which]

            @pl.when(jnp.logical_not(here) & (zl == zs))
            def _():
                last_copy(tile, group, zs).start()

    def pass_on(step, spot, part):
        here = slice(part * rows, (part + 1) * rows)
        chain_copy(step, part).wait_recv()
        chain_out[step, here] = (held[spot, here] + chain_in[step, here].astype(F32)).astype(BF16)
        chain_copy(step, part).start()

    def work_at(position):
        step = jnp.where(position < 2, position, -1)
        step = jnp.where((position >= 5) & (position < 7), position - 3, step)
        step = jnp.where((position >= 10) & (position < 18), position - 6, step)
        step = jnp.where(
            (position >= 18 + FLUSH) & (position < PRODUCTS + PAUSES), position - PAUSES, step
        )
        return step

    def tick(position, carry):
        step = work_at(position)
        slot, tile, group, away = split(jnp.maximum(step, 0))
        spot = lax.bitwise_and(position, 15)

        @pl.when(step == 2)
        def _():
            forward(1)

        @pl.when(step == 4)
        def _():
            forward(2)
            on_up(0).start()
            on_down(2).start()

        @pl.when(step == 6)
        def _():
            forward(3)
            on_up(1).start()
            on_down(3).start()

        @pl.when(position == 18 + FLUSH // 2)
        def _():
            forward_far(0)
            forward_far(2)

        @pl.when(step == 12)
        def _():
            forward_far(1)
            forward_far(3)

        @pl.when(step == 2)
        def _():
            for q in range(CHUNKS):
                act_wait(1, q)

        @pl.when(step == 12)
        def _():
            for q in range(CHUNKS):
                act_wait(4, q)
                act_wait(5, q)

        @pl.when(step == 27)
        def _():
            for q in range(CHUNKS):
                act_wait(7, q)

        @pl.when((step >= 0) & (tile == 0))
        def _():
            for q in range(CHUNKS):
                share_copy(slot, q).wait_recv()

        @pl.when(step == 0)
        def _():
            w_own.wait()
            w_others[0].wait_recv()

        @pl.when(step == 4)
        def _():
            w_others[1].wait_recv()
            w_others[2].wait_recv()

        @pl.when(step == 21)
        def _():
            w_others[3].wait_recv()
            w_others[4].wait_recv()

        @pl.when(step >= 0)
        def _():
            column = pl.ds(pl.multiple_of(lax.bitwise_and(tile, 1) * 256, 256), 256)
            held[spot] = jnp.dot(
                acts[slot], weights[lax.shift_right_arithmetic(tile, 1), :, column], preferred_element_type=F32
            )

            @pl.when(away == 1)
            def _():
                chain_out[step, 0:rows] = held[spot, 0:rows].astype(BF16)
                chain_copy(step, 0).start()

            @pl.when(away == 3)
            def _():
                chain_out[step, rows:] = held[spot, rows:].astype(BF16)
                chain_copy(step, 1).start()

        @pl.when(step == 0)
        def _():
            send_later(2)

        @pl.when(step == 1)
        def _():
            forward(0)
            send_later(3)

        two = work_at(position - HOP2)
        away_two = split(jnp.maximum(two, 0))[3]

        @pl.when((two >= 0) & (away_two == 2))
        def _():
            for part in range(2):
                pass_on(two, lax.bitwise_and(position + 16 - HOP2, 15), part)

        three = work_at(position - HOP3)
        away_three = split(jnp.maximum(three, 0))[3]

        @pl.when((three >= 0) & (away_three == 3))
        def _():
            pass_on(three, lax.bitwise_and(position + 16 - HOP3, 15), 0)

        @pl.when((three >= 0) & (away_three == 1))
        def _():
            pass_on(three, lax.bitwise_and(position + 16 - HOP3, 15), 1)

        four = work_at(position - HOP4)
        _, tile_four, group_four, away_four = split(jnp.maximum(four, 0))

        @pl.when((four >= 0) & (away_four == 0))
        def _():
            which = group_four * 4 + tile_four
            for part in range(2):
                chain_copy(four, part).wait_recv()
            last_out[which] = (
                held[lax.bitwise_and(position + 16 - HOP4, 15)] + chain_in[four].astype(F32)
            ).astype(BF16)
            send_last(tile_four, group_four)

        return carry

    lax.fori_loop(0, PRODUCTS + PAUSES + HOP4, tick, 0)

    for copy in w_others:
        copy.wait_send()
    for copy in kz_sends:
        copy.wait_send()
    all_of(kv.at[pl.ds(0, 12)], ky_send, ks_recv).wait_send()
    all_of(kv.at[pl.ds(0, 16)], ks_send, ks_recv).wait_send()
    for q in range(CHUNKS):
        if q >= 2:
            to_up(q).wait_send()
            to_down(q).wait_send()
        (on_up if q < CHUNKS // 2 else on_down)(q).wait_send()
    all_of(acts.at[pl.ds(0, 4), :, depth_here], y_send, ks_recv).wait_send()
    all_of(acts.at[:, :, depth_here], as_send, ks_recv).wait_send()
    all_of(chain_out.at[pl.ds(0, PRODUCTS // 4 * 3)], chain_send, ks_recv).wait_send()

    @pl.when(near == 1)
    def _():
        all_of(last_out.at[pl.ds(0, 6)], last_send, ks_recv).wait_send()

    @pl.when(near == 0)
    def _():
        all_of(last_out, last_send, ks_recv).wait_send()

    for zs in range(2):
        for cs in range(2):
            @pl.when((near == 0) | (zs != zl) | (cs != core))
            def _():
                for part in range(2):
                    column = cs * half + part * 256
                    remote(
                        last_out.at[0], (low_in, high_in)[zs].at[:, column:column + 256],
                        last_send, last_recv.at[zs * 2 + cs, part], sibling,
                    ).wait_recv()


def per_device(
    queries, key_states, value_states, vertical_blocks, slash_offsets, positions, out_weight
):
    tokens, depth = queries.shape
    width = out_weight.shape[1]
    half = width // 2
    inverse_freq = 500000.0 ** (-np.arange(HD // 2) * (2.0 / HD))
    freq = jnp.asarray(np.tile(inverse_freq, (8, 2)), F32)
    anywhere = pl.BlockSpec(memory_space=pl.ANY)
    dma = pltpu.SemaphoreType.DMA
    low, high = pl.pallas_call(
        kernel,
        out_shape=[jax.ShapeDtypeStruct((tokens, width), BF16)] * 2,
        in_specs=[anywhere] * 3 + [pl.BlockSpec(memory_space=pltpu.VMEM)] + [anywhere] * 4,
        out_specs=[pl.BlockSpec(memory_space=pltpu.VMEM)] * 2,
        scratch_shapes=[
            pltpu.SMEM(vertical_blocks.shape[::-1], jnp.int32),
            pltpu.SMEM(slash_offsets.shape[::-1], jnp.int32),
            pltpu.SMEM(positions.shape, jnp.int32),
            pltpu.VMEM((tokens, depth), BF16),
            pltpu.VMEM((BLK, HD), BF16),
            pltpu.VMEM((BLK, HD), BF16),
            pltpu.VMEM((2, depth // HD, HD, BLK), BF16),
            pltpu.VMEM((32, 2, BLK, HD), BF16),
            pltpu.VMEM((8, tokens, 2 * depth), BF16),
            pltpu.VMEM((2, 2 * depth, half), BF16),
            pltpu.VMEM((16, tokens, 256), F32),
            pltpu.VMEM((PRODUCTS, tokens, 256), BF16),
            pltpu.VMEM((PRODUCTS, tokens, 256), BF16),
            pltpu.VMEM((8, tokens, 256), BF16),
            dma((6,)), dma, dma((5,)), dma((5,)),
            dma((4,)), dma((4,)), dma, dma((4, 4)), dma, dma,
            dma((8, CHUNKS)), dma, dma((8, CHUNKS)), dma((3, CHUNKS)), dma,
            dma, dma((PRODUCTS, 2)), dma, dma((4, 2)),
        ],
        compiler_params=pltpu.CompilerParams(
            collective_id=0, has_side_effects=True, vmem_limit_bytes=56 * 1024 * 1024
        ),
    )(
        vertical_blocks.T, slash_offsets.T, positions, freq, queries, key_states, value_states,
        out_weight,
    )
    return (low.astype(F32) + high.astype(F32)).astype(BF16)


def solution(mesh):
    placed = (
        P("ctx", "head"),
        P("ctx", None),
        P("ctx", None),
        P("head", None),
        P("head", None),
        P("ctx"),
        P("head", "ctx"),
    )
    return jax.shard_map(
        per_device, mesh=mesh, in_specs=placed, out_specs=P("head", "ctx"), check_vma=False
    )
```

```python
import math

import jax
import jax.numpy as jnp
import numpy as np
from jax import lax
from jax.experimental import pallas as pl
from jax.experimental.pallas import tpu as pltpu
from jax.sharding import PartitionSpec as P

HD = 128
BLK = 128
MESH = pl.DeviceIdType.MESH
BF16 = jnp.bfloat16
F32 = jnp.float32

HOP2, HOP3, HOP4 = 4, 9, 14
PRODUCTS = 32
FLUSH = 2
PAUSES = 6 + FLUSH
CHUNKS = 4


def place():
    ctx = lax.axis_index("ctx")
    head = lax.axis_index("head")
    return ctx // 4, ctx % 4, head // 4, (head // 2) % 2, head % 2


def device(zh, y, x, zl, core):
    return {"ctx": (zh % 4) * 4 + y % 4, "head": (x % 4) * 4 + zl * 2 + core}


def remote(src, dst, send, recv, where):
    return pltpu.make_async_remote_copy(
        src_ref=src, dst_ref=dst, send_sem=send, recv_sem=recv, device_id=where, device_id_type=MESH
    )


def turned(states, cosine, sine):
    states = states.astype(F32)
    return states * cosine + pltpu.roll(states, HD // 2, 1) * sine


def kernel(
    vert_in, slash_in, pos_in, freq_ref, q_in, k_ref, v_ref, w_ref, low_in, high_in,
    vert_ref, slash_ref, pos_ref, q_ref, k_own, v_own, q_rot, kv, acts, weights, held, chain_out,
    chain_in, last_out,
    own_sem, w_sem, w_send, w_recv, kz_send, kz_recv, ky_send, ky_recv, ks_send, ks_recv,
    act_recv, as_send, as_recv, z_send, y_send, chain_send, chain_recv, last_send, last_recv,
):
    zh, y, x, zl, core = place()
    mate = 3 - y
    pair = y + 1 - 2 * (y % 2)
    z_up = device(zh + 1, y, x, zl, core)
    z_down = device(zh + 3, y, x, zl, core)
    y_up = device(zh, y + 1, x, zl, core)
    y_down = device(zh, y + 3, x, zl, core)
    y_mate = device(zh, mate, x, zl, core)
    y_pair = device(zh, pair, x, zl, core)
    y_pair_sibling = device(zh, pair, x, zl, 1 - core)
    x_up = device(zh, y, x + 1, zl, core)
    x_down = device(zh, y, x + 3, zl, core)
    sibling = device(zh, y, x, zl, 1 - core)
    half = weights.shape[2]
    depth = q_ref.shape[1]
    rows = acts.shape[1] // 2
    chunk = acts.shape[1] // CHUNKS
    heads = q_ref.shape[1] // HD

    kv_column = pl.multiple_of((x * 2 + zl) * HD, HD)
    own_rows = pl.ds(pl.multiple_of(core * BLK, BLK), BLK)
    small = [
        pltpu.make_async_copy(src, dst, own_sem.at[i])
        for i, (src, dst) in enumerate((
            (pos_in, pos_ref),
            (k_ref.at[own_rows, pl.ds(kv_column, HD)], k_own),
            (v_ref.at[own_rows, pl.ds(kv_column, HD)], v_own),
            (q_in, q_ref),
            (vert_in, vert_ref),
            (slash_in, slash_ref),
        ))
    ]
    for copy in small:
        copy.start()

    depth_here = pl.ds(pl.multiple_of(core * depth, depth), depth)

    def w_part(which, start=0, size=half):
        return w_ref.at[:, pl.ds(pl.multiple_of(which * half + start, 256), size)]

    w_own = pltpu.make_async_copy(w_part(core), weights.at[0, depth_here], w_sem)
    w_others = [remote(w_part(1 - core), weights.at[0, depth_here], w_send.at[0], w_recv.at[0], sibling)]
    for start in (0, 256):
        for which, where in ((core, y_pair), (1 - core, y_pair_sibling)):
            i = len(w_others)
            w_others.append(remote(
                w_part(which, start, 256), weights.at[1, depth_here, pl.ds(start, 256)],
                w_send.at[i], w_recv.at[i], where,
            ))
    w_own.start()

    token_row = zl * 2 + core
    near = jnp.where((token_row == y) | (token_row == mate), 1, 0)
    source_row = jnp.where(near == 1, y, pair)

    barrier = pltpu.get_barrier_semaphore()

    def greet(where):
        pl.semaphore_signal(barrier, inc=1, device_id=where, device_id_type=MESH)

    for where in (z_up, z_down, y_up, y_down, x_up, x_down, sibling, y_pair_sibling):
        greet(where)
    for zs in range(2):
        for cs in range(2):
            @pl.when((near == 0) | (zs != zl) | (cs != core))
            def _():
                greet(device(zh, source_row, x, zs, cs))

    def block(dz, dy, which=core):
        return (((zh + dz) % 4) * 4 + (y + dy) % 4) * 2 + which

    mine = block(0, 0)
    small[0].wait()
    lane = lax.broadcasted_iota(jnp.int32, (BLK, HD), 1)
    row = lax.broadcasted_iota(jnp.int32, (BLK, HD), 0)
    first = lane < HD // 2
    start = jnp.where(first, pos_ref[0], pos_ref[BLK])
    angles = (start + row).astype(F32) * freq_ref[0:1, :]
    cosine = jnp.cos(angles)
    sine = jnp.sin(angles)
    cosine_other = pltpu.roll(cosine, HD // 2, 1)
    sine_other = pltpu.roll(sine, HD // 2, 1)
    tables = (
        (jnp.where(first, cosine, cosine_other), jnp.where(first, -sine, sine_other)),
        (jnp.where(first, cosine_other, cosine), jnp.where(first, -sine_other, sine)),
    )
    small[1].wait()
    small[2].wait()
    kv[mine, 0] = turned(
        k_own[...], *(jnp.where(core == 0, one, two) for one, two in zip(*tables))
    ).astype(BF16)
    kv[mine, 1] = v_own[...].astype(F32).T.astype(BF16)
    pl.semaphore_wait(barrier, 12 - near)

    def all_of(ref, send, recv):
        return remote(ref, ref, send, recv, sibling)

    def kz_copy(dz_there, index, where):
        return remote(kv.at[mine], kv.at[mine], kz_send.at[index], kz_recv.at[dz_there], where)

    def kz_on(dz, part, where):
        here = kv.at[block(dz, 0), part]
        return remote(here, here, kz_send.at[2 + part], kz_recv.at[2 + part], where)

    def ky_copy(dz, dy, index, there, where):
        here = kv.at[block(dz, dy)]
        return remote(here, here, ky_send, ky_recv.at[dz, there], where)

    def ks_copy(dz, dy):
        here = kv.at[block(dz, dy)]
        return remote(here, here, ks_send, ks_recv, sibling)

    def kv_row(dz):
        return (ky_copy(dz, 0, 0, 3, y_up), ky_copy(dz, 0, 1, 1, y_down), ks_copy(dz, 0))

    def kv_far(dz):
        if dz < 2:
            return ky_copy(dz, 3, 2, 2, y_up)
        return ky_copy(dz, 1, 2, 2, y_down)

    kz_sends = (kz_copy(1, 0, z_up), kz_copy(0, 1, z_down), kz_on(3, 0, z_up), kz_on(1, 1, z_down))
    kz_sends[0].start()
    kz_sends[1].start()
    for copy in kv_row(0):
        copy.start()

    scale = math.log2(math.e) / math.sqrt(HD)
    small[3].wait()
    for part in range(2):
        cosine, sine = (table * scale for table in tables[part])
        for h in range(heads):
            states = q_ref[part * BLK:(part + 1) * BLK, h * HD:(h + 1) * HD]
            q_rot[part, h] = turned(states, cosine, sine).T.astype(BF16)
    small[4].wait()
    small[5].wait()

    kz_sends[1].wait_recv()
    kz_sends[3].start()
    for copy in kv_row(1):
        copy.start()
    kz_sends[0].wait_recv()
    kz_sends[2].start()
    for copy in kv_row(3):
        copy.start()

    def kv_near(dz):
        for dy in (3, 1):
            ky_copy(dz, dy, 0, dy, sibling).wait_recv()
            if (dy == 3) == (dz < 2):
                kv_far(dz).start()
            ks_copy(dz, dy).start()

    kv_near(0)
    kz_sends[2].wait_recv()
    kz_sends[3].wait_recv()
    for copy in kv_row(2):
        copy.start()
    kv_near(1)
    kv_near(3)
    kv_near(2)
    for copy in w_others:
        copy.start()
    for dz in range(4):
        ky_copy(dz, 2, 0, 2, sibling).wait_recv()
        ks_copy(dz, 2).start()
    all_of(kv.at[pl.ds(0, 16)], ks_send, ks_recv).wait_recv()

    def act_at(slot, part):
        return acts.at[slot, pl.ds(part * chunk, chunk), depth_here]

    def act_copy(src_slot, dst_slot, part, send, where):
        return remote(
            act_at(src_slot, part), act_at(dst_slot, part), send, act_recv.at[dst_slot, part], where
        )

    def share_copy(slot, part):
        here = act_at(slot, part)
        return remote(here, here, as_send, as_recv.at[slot, part], sibling)

    def act_wait(slot, part):
        act_copy(slot, slot, part, z_send.at[0, 0], sibling).wait_recv()
        share_copy(slot, part).start()

    to_up = lambda part: act_copy(0, 3, part, z_send.at[0, part], z_up)
    to_down = lambda part: act_copy(0, 2, part, z_send.at[1, part], z_down)
    on_up = lambda part: act_copy(3, 6, part, z_send.at[2, part], z_up)
    on_down = lambda part: act_copy(2, 6, part, z_send.at[2, part], z_down)
    y_slot = {0: 1, 2: 4, 3: 5, 6: 7}
    to_mate = lambda slot, part: act_copy(slot, y_slot[slot], part, y_send, y_mate)

    ctx = zh * 4 + y

    def attend(part):
        here = ctx * 2 + part

        def one_head(h, carry):
            column = pl.ds(pl.multiple_of(core * depth + h * HD, HD), HD)
            vertical = [vert_ref[s, h] for s in range(4)]
            blocks = [here] + vertical
            bias = [None] + [jnp.where(b < here, 0.0, -1e30) for b in vertical]
            for s in range(1, 4):
                b = here - slash_ref[s, h]
                seen = (b == vertical[0]) | (b == vertical[1]) | (b == vertical[2]) | (b == vertical[3])
                blocks.append(jnp.maximum(b, 0))
                bias.append(jnp.where((b >= 0) & jnp.logical_not(seen), 0.0, -1e30))
            keys = jnp.concatenate([kv[b, 0] for b in blocks], axis=0)
            values = jnp.concatenate([kv[b, 1] for b in blocks], axis=1)
            scores = jnp.dot(keys, q_rot[part, h], preferred_element_type=F32)
            tiles_of = [scores[s * BLK:(s + 1) * BLK] for s in range(8)]
            key_row = lax.broadcasted_iota(jnp.int32, (BLK, BLK), 0)
            query_row = lax.broadcasted_iota(jnp.int32, (BLK, BLK), 1)
            tiles_of[0] = jnp.where(key_row <= query_row, tiles_of[0], -1e30)
            top = jnp.max(tiles_of[0], axis=0, keepdims=True)
            for s in range(1, 8):
                top = jnp.maximum(top, jnp.max(tiles_of[s], axis=0, keepdims=True) + bias[s])
            powers = [jnp.exp2(tiles_of[0] - top)]
            for s in range(1, 8):
                powers.append(jnp.exp2(tiles_of[s] - (top - bias[s])))
            total = sum(jnp.sum(p, axis=0, keepdims=True) for p in powers)
            mixed = jnp.dot(
                values, jnp.concatenate([p.astype(BF16) for p in powers], axis=0),
                preferred_element_type=F32,
            )
            acts[0, part * BLK:(part + 1) * BLK, column] = (mixed * (1.0 / total)).T.astype(BF16)
            return carry

        lax.fori_loop(0, heads, one_head, 0, unroll=8)

    for part in range(2):
        attend(part)
        to_up(part).start()
        to_down(part).start()
        for q in (2 * part, 2 * part + 1):
            to_mate(0, q).start()
            share_copy(0, q).start()

    def send_later(q):
        to_up(q - 2).wait_send()
        to_down(q - 2).wait_send()
        to_up(q).start()
        to_down(q).start()

    def forward(q):
        act_wait(3, q)
        to_mate(3, q).start()
        act_wait(2, q)
        to_mate(2, q).start()

    def forward_far(q):
        act_wait(6, q)
        to_mate(6, q).start()

    def split(step):
        third = lax.shift_right_arithmetic((step - 6) * 11, 5)
        slot = jnp.where(step < 4, lax.shift_right_arithmetic(step, 1), step - 4)
        tile = jnp.where(step < 4, lax.bitwise_and(step, 1), 2)
        slot = jnp.where(step >= 6, 2 + third, slot)
        tile = jnp.where(step >= 6, step - 6 - 3 * third, tile)
        slot = jnp.where(step >= 21, step - 21, slot)
        tile = jnp.where(step >= 21, 3, tile)
        slot = jnp.where(step >= 28, 7, slot)
        tile = jnp.where(step >= 28, step - 28, tile)
        ahead = jnp.where(slot < 2, 0, jnp.where(slot < 6, 1 + 2 * lax.bitwise_and(slot, 1), 2))
        group = jnp.where(
            slot < 2, slot, jnp.where(slot < 6, lax.shift_right_arithmetic(slot - 2, 1), slot - 6)
        )
        return slot, tile, group, lax.bitwise_and(x + 8 - zh - ahead, 3)

    def chain_copy(step, part):
        here = pl.ds(part * rows, rows)
        return remote(
            chain_out.at[step, here], chain_in.at[step, here], chain_send,
            chain_recv.at[step, part], x_down if part else x_up,
        )

    def last_place(tile, group):
        row = jnp.where(group == 0, y, mate)
        column = jnp.where(tile < 2, y, pair)
        here = (tile < 2) & (row // 2 == zl) & (row % 2 == core)
        columns = pl.ds(pl.multiple_of(core * half + (tile % 2) * 256, 256), 256)
        return here, device(zh, column, x, row // 2, row % 2), group * 4 + tile, columns

    def last_copy(tile, group, zs):
        _, where, which, columns = last_place(tile, group)
        return remote(
            last_out.at[which], (low_in, high_in)[zs].at[:, columns], last_send,
            last_recv.at[zs * 2 + core, tile % 2], where,
        )

    def send_last(tile, group):
        here, _, which, columns = last_place(tile, group)
        for zs, target in enumerate((low_in, high_in)):
            @pl.when(here & (zl == zs))
            def _():
                target[:, columns] = last_out[which]

            @pl.when(jnp.logical_not(here) & (zl == zs))
            def _():
                last_copy(tile, group, zs).start()

    def pass_on(step, spot, part):
        here = slice(part * rows, (part + 1) * rows)
        chain_copy(step, part).wait_recv()
        chain_out[step, here] = (held[spot, here] + chain_in[step, here].astype(F32)).astype(BF16)
        chain_copy(step, part).start()

    def work_at(position):
        step = jnp.where(position < 2, position, -1)
        step = jnp.where((position >= 5) & (position < 7), position - 3, step)
        step = jnp.where((position >= 10) & (position < 18), position - 6, step)
        step = jnp.where(
            (position >= 18 + FLUSH) & (position < PRODUCTS + PAUSES), position - PAUSES, step
        )
        return step

    def tick(position, carry):
        step = work_at(position)
        slot, tile, group, away = split(jnp.maximum(step, 0))
        spot = lax.bitwise_and(position, 15)

        two = work_at(position - HOP2)
        away_two = split(jnp.maximum(two, 0))[3]

        @pl.when((two >= 0) & (away_two == 2))
        def _():
            for part in range(2):
                pass_on(two, lax.bitwise_and(position + 16 - HOP2, 15), part)

        three = work_at(position - HOP3)
        away_three = split(jnp.maximum(three, 0))[3]

        @pl.when((three >= 0) & (away_three == 3))
        def _():
            pass_on(three, lax.bitwise_and(position + 16 - HOP3, 15), 0)

        @pl.when((three >= 0) & (away_three == 1))
        def _():
            pass_on(three, lax.bitwise_and(position + 16 - HOP3, 15), 1)

        four = work_at(position - HOP4)
        _, tile_four, group_four, away_four = split(jnp.maximum(four, 0))

        @pl.when((four >= 0) & (away_four == 0))
        def _():
            which = group_four * 4 + tile_four
            for part in range(2):
                chain_copy(four, part).wait_recv()
            last_out[which] = (
                held[lax.bitwise_and(position + 16 - HOP4, 15)] + chain_in[four].astype(F32)
            ).astype(BF16)
            send_last(tile_four, group_four)

        @pl.when(step == 2)
        def _():
            forward(1)

        @pl.when(step == 4)
        def _():
            forward(2)
            on_up(0).start()
            on_down(2).start()

        @pl.when(step == 6)
        def _():
            forward(3)
            on_up(1).start()
            on_down(3).start()

        @pl.when(position == 18 + FLUSH // 2)
        def _():
            forward_far(0)
            forward_far(2)

        @pl.when(step == 12)
        def _():
            forward_far(1)
            forward_far(3)

        @pl.when(step == 2)
        def _():
            for q in range(CHUNKS):
                act_wait(1, q)

        @pl.when(step == 12)
        def _():
            for q in range(CHUNKS):
                act_wait(4, q)
                act_wait(5, q)

        @pl.when(step == 27)
        def _():
            for q in range(CHUNKS):
                act_wait(7, q)

        @pl.when((step >= 0) & (tile == 0))
        def _():
            for q in range(CHUNKS):
                share_copy(slot, q).wait_recv()

        @pl.when(step == 0)
        def _():
            w_own.wait()
            w_others[0].wait_recv()

        @pl.when(step == 4)
        def _():
            w_others[1].wait_recv()
            w_others[2].wait_recv()

        @pl.when(step == 21)
        def _():
            w_others[3].wait_recv()
            w_others[4].wait_recv()

        @pl.when(step >= 0)
        def _():
            column = pl.ds(pl.multiple_of(lax.bitwise_and(tile, 1) * 256, 256), 256)
            held[spot] = jnp.dot(
                acts[slot], weights[lax.shift_right_arithmetic(tile, 1), :, column], preferred_element_type=F32
            )

            @pl.when(away == 1)
            def _():
                chain_out[step, 0:rows] = held[spot, 0:rows].astype(BF16)
                chain_copy(step, 0).start()

            @pl.when(away == 3)
            def _():
                chain_out[step, rows:] = held[spot, rows:].astype(BF16)
                chain_copy(step, 1).start()

        @pl.when(step == 0)
        def _():
            send_later(2)

        @pl.when(step == 1)
        def _():
            forward(0)
            send_later(3)

        return carry

    lax.fori_loop(0, PRODUCTS + PAUSES + HOP4, tick, 0)

    for copy in w_others:
        copy.wait_send()
    for copy in kz_sends:
        copy.wait_send()
    all_of(kv.at[pl.ds(0, 12)], ky_send, ks_recv).wait_send()
    all_of(kv.at[pl.ds(0, 16)], ks_send, ks_recv).wait_send()
    for q in range(CHUNKS):
        if q >= 2:
            to_up(q).wait_send()
            to_down(q).wait_send()
        (on_up if q < CHUNKS // 2 else on_down)(q).wait_send()
    all_of(acts.at[pl.ds(0, 4), :, depth_here], y_send, ks_recv).wait_send()
    all_of(acts.at[:, :, depth_here], as_send, ks_recv).wait_send()
    all_of(chain_out.at[pl.ds(0, PRODUCTS // 4 * 3)], chain_send, ks_recv).wait_send()

    @pl.when(near == 1)
    def _():
        all_of(last_out.at[pl.ds(0, 6)], last_send, ks_recv).wait_send()

    @pl.when(near == 0)
    def _():
        all_of(last_out, last_send, ks_recv).wait_send()

    for zs in range(2):
        for cs in range(2):
            @pl.when((near == 0) | (zs != zl) | (cs != core))
            def _():
                for part in range(2):
                    column = cs * half + part * 256
                    remote(
                        last_out.at[0], (low_in, high_in)[zs].at[:, column:column + 256],
                        last_send, last_recv.at[zs * 2 + cs, part], sibling,
                    ).wait_recv()


def per_device(
    queries, key_states, value_states, vertical_blocks, slash_offsets, positions, out_weight
):
    tokens, depth = queries.shape
    width = out_weight.shape[1]
    half = width // 2
    inverse_freq = 500000.0 ** (-np.arange(HD // 2) * (2.0 / HD))
    freq = jnp.asarray(np.tile(inverse_freq, (8, 2)), F32)
    anywhere = pl.BlockSpec(memory_space=pl.ANY)
    dma = pltpu.SemaphoreType.DMA
    low, high = pl.pallas_call(
        kernel,
        out_shape=[jax.ShapeDtypeStruct((tokens, width), BF16)] * 2,
        in_specs=[anywhere] * 3 + [pl.BlockSpec(memory_space=pltpu.VMEM)] + [anywhere] * 4,
        out_specs=[pl.BlockSpec(memory_space=pltpu.VMEM)] * 2,
        scratch_shapes=[
            pltpu.SMEM(vertical_blocks.shape[::-1], jnp.int32),
            pltpu.SMEM(slash_offsets.shape[::-1], jnp.int32),
            pltpu.SMEM(positions.shape, jnp.int32),
            pltpu.VMEM((tokens, depth), BF16),
            pltpu.VMEM((BLK, HD), BF16),
            pltpu.VMEM((BLK, HD), BF16),
            pltpu.VMEM((2, depth // HD, HD, BLK), BF16),
            pltpu.VMEM((32, 2, BLK, HD), BF16),
            pltpu.VMEM((8, tokens, 2 * depth), BF16),
            pltpu.VMEM((2, 2 * depth, half), BF16),
            pltpu.VMEM((16, tokens, 256), F32),
            pltpu.VMEM((PRODUCTS, tokens, 256), BF16),
            pltpu.VMEM((PRODUCTS, tokens, 256), BF16),
            pltpu.VMEM((8, tokens, 256), BF16),
            dma((6,)), dma, dma((5,)), dma((5,)),
            dma((4,)), dma((4,)), dma, dma((4, 4)), dma, dma,
            dma((8, CHUNKS)), dma, dma((8, CHUNKS)), dma((3, CHUNKS)), dma,
            dma, dma((PRODUCTS, 2)), dma, dma((4, 2)),
        ],
        compiler_params=pltpu.CompilerParams(
            collective_id=0, has_side_effects=True, vmem_limit_bytes=56 * 1024 * 1024
        ),
    )(
        vertical_blocks.T, slash_offsets.T, positions, freq, queries, key_states, value_states,
        out_weight,
    )
    return (low.astype(F32) + high.astype(F32)).astype(BF16)


def solution(mesh):
    placed = (
        P("ctx", "head"),
        P("ctx", None),
        P("ctx", None),
        P("head", None),
        P("head", None),
        P("ctx"),
        P("head", "ctx"),
    )
    return jax.shard_map(
        per_device, mesh=mesh, in_specs=placed, out_specs=P("head", "ctx"), check_vma=False
    )
```
